512 devices in a mesh: date: 16 (over z, x_hi), trade: 16 (over y, core), path: 2 (over x_lo).
Axes of the slice: x: 4 (x_hi: 2, x_lo: 2; x = x_hi * 2 + x_lo), y: 8, z: 8, core: 2. Of those that a mesh axis runs over, the one named last changes fastest.
Arguments:
- normals: bfloat16 [32, 64, 8192], P('date', None, ('trade', 'path')), may hold values from -6 to 6
- chol: float32 [64, 64], replicated, as said below
- volatility: float32 [64], replicated, may hold values from 0.5 to 2
- start_state: float32 [64], replicated, may hold values from -3 to 3
- basis_map: float32 [64, 128], replicated, may hold values from -0.75 to 0.75
- basis_bias: float32 [128], replicated, may hold values from -3 to 3
- coef: bfloat16 [128, 16384], P(None, 'trade'), may hold values from -0.5 to 0.5
- maturity: int32 [16384], P('trade'), may hold values from 1 to 32
- netting: int32 [16384], P('trade'), may hold values from 0 to 2047, as said below
Outputs:
- exposure: float32 [32, 2048], P('date', 'trade')
The draws below stay inside these ranges and needn't reach their ends.
Inputs may be any that keep to these rules, and one draw needn't show every extreme that they name: netting sets are whole within a shard of trades: netting[j] // 128 == j // 1024, and every netting set holds at least one trade. `chol`: lower triangular with a positive diagonal.
All inputs are finite; a program needn't handle non-finite values.
Results may differ from the reference program's by a relative error of at most 0.00035.
Values may be sent and summed in bfloat16 or wider, within the bound.
A program may use at most 64 MiB of HBM per device.

```python
import math
import jax
import jax.numpy as jnp
from jax import lax

F = 64
K = 128
TR_DEV = 1024
NS_DEV = 128
DATES = 32
PATHS = 8192
TRADES = 16384
NSETS = 2048


def draw_chol(key, part):
    first = jax.random.fold_in(key, 11)
    second = jax.random.fold_in(key, 12)
    spread = jax.random.normal(first, (F, F), jnp.float32) * (0.6 / jnp.sqrt(jnp.float32(F)))
    diag_vals = jax.random.uniform(second, (F,), jnp.float32, 0.7, 1.2)
    return jnp.tril(spread, -1) + jnp.diag(diag_vals)


def draw_netting(key, part):
    first = jax.random.fold_in(key, 21)
    index = jnp.arange(TRADES, dtype=jnp.int32)
    local = index % TR_DEV
    picked = jax.random.randint(first, (TRADES,), 0, NS_DEV, dtype=jnp.int32)
    inside = jnp.where(local < NS_DEV, local, picked)
    return index // TR_DEV * NS_DEV + inside


def touch_ends(entries, own_key, least, largest):
    longest = entries.shape.index(max(entries.shape))
    spots = []
    for shift in (0, 1):
        where = [jax.random.randint(jax.random.fold_in(own_key, axis), (), 0, length) for axis, length in enumerate(entries.shape)]
        where[longest] = (where[longest] + shift) % entries.shape[longest]
        spots.append(tuple(where))
    return entries.at[spots[0]].set(least).at[spots[1]].set(largest)


def shard_levels(own_key, dims, split, smallest, top_value):
    def one(position, parts):
        draws = jax.random.uniform(jax.random.fold_in(jax.random.fold_in(own_key, 6), position), (parts,), jnp.float32, smallest / len(split), top_value / len(split))
        return jnp.repeat(jnp.exp(draws), dims[position] // parts).reshape((-1,) + (1,) * (len(dims) - position - 1))

    loudness = one(*split[0])
    for cut in split[1:]:
        loudness = loudness * one(*cut)
    return loudness


def bell_draw(stream_key, shape, scale, reach, pieces=(), kind=jnp.bfloat16):
    result = scale * jax.random.normal(stream_key, shape, jnp.float32)
    if pieces:
        result = result * shard_levels(stream_key, shape, pieces, -0.22, 0.18)
    return jnp.clip(result, -reach, reach).astype(kind)


def setup_inputs(seed: int = 0) -> dict:
    streams_of = jax.random.split(jax.random.key(seed), 10)
    return {
        "normals": bell_draw(streams_of[0], (DATES, F, PATHS), 1.0, 6.0, ((0, 16), (2, 32))),
        "chol": draw_chol(jax.random.fold_in(streams_of[9], 71), 0),
        "volatility": jnp.clip(jnp.exp(jax.random.uniform(streams_of[2], (F,), jnp.float32, math.log(0.5), math.log(2.0))), 0.5, 2.0),
        "start_state": bell_draw(streams_of[3], (F,), 0.5, 3.0, (), jnp.float32),
        "basis_map": bell_draw(streams_of[4], (F, K), F ** -0.5, 0.75, (), jnp.float32),
        "basis_bias": bell_draw(streams_of[5], (K,), 0.5, 3.0, (), jnp.float32),
        "coef": bell_draw(streams_of[6], (K, TRADES), K ** -0.5, 0.5, ((1, 16),)),
        "maturity": touch_ends(jax.random.randint(streams_of[7], (TRADES,), 1, DATES + 1), jax.random.fold_in(streams_of[7], 1), 1, DATES).astype(jnp.int32),
        "netting": draw_netting(jax.random.fold_in(streams_of[9], 71), 0),
    }


def reference(normals, chol, volatility, start_state, basis_map, basis_bias, coef, maturity, netting):
    scale = volatility * jnp.sqrt(jnp.float32(1.0) / DATES)
    moves = jnp.einsum('fg,tgp->tfp', chol, normals.astype(jnp.float32), precision=lax.Precision.HIGHEST)
    increment = moves * scale[None, :, None]
    state = start_state[None, :, None] + jnp.cumsum(increment, axis=0)
    coef_wide = coef.astype(jnp.float32)
    date_ids = jnp.arange(DATES, dtype=jnp.int32)

    def one_date(args):
        slab, when = args
        pre = jnp.dot(slab.T, basis_map, precision=lax.Precision.HIGHEST) + basis_bias[None, :]
        basis = jnp.tanh(pre).astype(jnp.bfloat16)
        value = jnp.dot(basis.astype(jnp.float32), coef_wide, precision=lax.Precision.HIGHEST)
        alive = (when < maturity).astype(jnp.float32)
        value = (value * alive[None, :]).astype(jnp.bfloat16)
        net = jax.ops.segment_sum(value.astype(jnp.float32).T, netting, NSETS)
        return lax.optimization_barrier(jnp.sum(jnp.maximum(net, 0.0), axis=1)) / PATHS
    return lax.map(one_date, (state, date_ids))
```

```python
import jax
import jax.numpy as jnp
import numpy as np
from jax import lax
from jax.experimental import pallas as pl
from jax.experimental.pallas import tpu as pltpu
from jax.sharding import PartitionSpec as P

MESH = pl.DeviceIdType.MESH
ND = 16
NB = 2
F = 64
K = 128
SETS = 128
SLICE = 16
NJ = 4
HIGH = lax.Precision.HIGHEST


def kernel(
    normals, chol, vol, start, bmap, bias, coef, mat, net,
    out,
    v_norm, v_chol, v_vol, v_start, v_bmap, v_bias, v_coef, v_mat, v_net,
    nt, arrived, sums, zbuf, cbuf, wbuf, part, fin,
    load_sem, send_sem, recv_sem, c_sem,
):
    d, t, p = lax.axis_index("date"), lax.axis_index("trade"), lax.axis_index("path")
    y, c = lax.div(t, 2), lax.rem(t, 2)
    j, par = lax.div(y, 2), lax.rem(y, 2)
    c1, p1 = 1 - c, 1 - p
    twin = t + 2 - 4 * par

    barrier = pltpu.get_barrier_semaphore()

    def hello(where):
        pl.semaphore_signal(barrier, inc=1, device_id=where, device_id_type=MESH)

    def hello_date(i, carry):
        hello({"date": lax.rem(d + i, ND)})
        return carry

    lax.fori_loop(1, ND, hello_date, 0)
    for i in range(1, NJ):
        hello({"trade": lax.rem(t + 4 * i, 16)})
    hello({"trade": twin})
    other = t + 1 - 2 * c
    hello({"trade": other})
    hello({"path": p1})
    hello({"trade": other, "path": p1})

    loads = [
        pltpu.make_async_copy(a, b, load_sem.at[i])
        for i, (a, b) in enumerate(
            (
                (normals, v_norm), (coef, v_coef), (mat, v_mat), (net, v_net), (chol, v_chol),
                (vol, v_vol), (start, v_start), (bmap, v_bmap), (bias, v_bias),
            )
        )
    ]
    for load in loads:
        load.start()

    loads[0].wait()
    flat = v_norm[...].reshape(NB * F, ND * SLICE).astype(jnp.float32)
    nt[...] = flat.T.astype(jnp.bfloat16).reshape(ND, SLICE, NB * F)
    arrived[d] = nt[d]

    for load in loads[1:4]:
        load.wait()
    local_set = v_net[...] - t * SETS
    trades = v_coef.shape[1]
    member = (lax.broadcasted_iota(jnp.int32, (SETS, trades), 0) == local_set)
    member = member.astype(jnp.float32).astype(jnp.bfloat16)
    for b in range(NB):
        alive = (d * NB + b < v_mat[...]).astype(jnp.float32).astype(jnp.bfloat16)
        folded = lax.dot_general(
            v_coef[...] * alive, member, (((1,), (1,)), ((), ())), preferred_element_type=jnp.float32
        )
        high = folded.astype(jnp.bfloat16)
        cbuf[j, c, b, :K, :] = high
        cbuf[j, c, b, K:, :] = (folded - high.astype(jnp.float32)).astype(jnp.bfloat16)

    pl.semaphore_wait(barrier, ND - 1 + NJ - 1 + 4)

    def slice_copy(e):
        return pltpu.make_async_remote_copy(
            src_ref=nt.at[e], dst_ref=arrived.at[d], send_sem=send_sem.at[0], recv_sem=recv_sem.at[0],
            device_id={"date": e}, device_id_type=MESH,
        )

    def send_slice(i, carry):
        slice_copy(lax.rem(d + i, ND)).start()
        return carry

    lax.fori_loop(1, ND, send_slice, 0)

    c_copies = [
        pltpu.make_async_remote_copy(
            src_ref=cbuf.at[j, c], dst_ref=cbuf.at[j, c], send_sem=send_sem.at[1], recv_sem=c_sem.at[i - 1],
            device_id={"trade": lax.rem(t + 4 * i, 16)}, device_id_type=MESH,
        )
        for i in range(1, NJ)
    ]
    for copy in c_copies:
        copy.start()

    def pass_on(slot):
        return pltpu.make_async_remote_copy(
            src_ref=cbuf.at[slot, c], dst_ref=cbuf.at[slot, c], send_sem=send_sem.at[2], recv_sem=recv_sem.at[2],
            device_id={"trade": other}, device_id_type=MESH,
        )

    pass_on(j).start()

    for load in loads[4:]:
        load.wait()
    scale = v_vol[...] * np.float32(np.sqrt(np.float32(1.0) / np.float32(ND * NB)))
    joint = jnp.dot(v_chol[...].T * scale, v_bmap[...], precision=HIGH, preferred_element_type=jnp.float32)
    offset = jnp.dot(v_start[...], v_bmap[...], precision=HIGH, preferred_element_type=jnp.float32) + v_bias[...]
    joint_high = joint.astype(jnp.bfloat16)
    joint_low = (joint - joint_high.astype(jnp.float32)).astype(jnp.bfloat16)
    wbuf[...] = jnp.zeros_like(wbuf)
    for b in range(NB):
        wbuf[pl.ds(b * F, F), pl.ds(b * K, K)] = joint_high
        wbuf[pl.ds(NB * F + b * F, F), pl.ds(b * K, K)] = joint_low
    offsets = jnp.concatenate([offset, offset], axis=1)

    def bytes_of(ref, sem, send):
        whole = pltpu.make_async_remote_copy(
            src_ref=ref, dst_ref=ref, send_sem=sem, recv_sem=sem, device_id={"trade": other}, device_id_type=MESH
        )
        return whole.wait_send() if send else whole.wait_recv()

    bytes_of(arrived.at[pl.ds(0, ND - 1)], recv_sem.at[0], False)
    later_half = lax.broadcasted_iota(jnp.int32, (SLICE, NB * F), 1) >= F
    total = jnp.zeros((SLICE, NB * F), jnp.float32)
    for e in range(ND):
        block = arrived[e].astype(jnp.float32)
        swapped = pltpu.roll(block, F, axis=1)
        pair = block + swapped
        sums[e] = (total + jnp.where(later_half, pair, block)).astype(jnp.bfloat16)
        total = total + pair

    def sums_copy(e, where):
        return pltpu.make_async_remote_copy(
            src_ref=sums.at[e], dst_ref=zbuf.at[par * ND + d], send_sem=send_sem.at[3], recv_sem=recv_sem.at[3],
            device_id={"date": e, "trade": where}, device_id_type=MESH,
        )

    def send_sums(i, carry):
        e = lax.rem(d + i, ND)
        sums_copy(e, t).start()
        sums_copy(e, twin).start()
        return carry

    lax.fori_loop(1, ND, send_sums, 0)
    sums_copy(d, twin).start()
    zbuf[par * ND + d] = sums[d]

    for i in range(1, NJ):
        c_copies[i - 1].wait_recv()
        pass_on(lax.rem(j + NJ - i, NJ)).start()

    bytes_of(zbuf.at[pl.ds(0, 2 * ND - 1)], recv_sem.at[3], False)
    z = zbuf[...].reshape(2 * ND * SLICE, NB * F)
    pre = jnp.dot(jnp.concatenate([z, z], axis=1), wbuf[...], preferred_element_type=jnp.float32)
    basis = jnp.tanh(pre + offsets).astype(jnp.bfloat16)

    bytes_of(cbuf.at[:, c1], recv_sem.at[2], False)
    for b in range(NB):
        own = basis[:, b * K : (b + 1) * K]
        twice = jnp.concatenate([own, own], axis=1)
        for slot in range(NJ):
            both = jnp.concatenate([cbuf[slot, 0, b], cbuf[slot, 1, b]], axis=1)
            values = jnp.dot(twice, both, preferred_element_type=jnp.float32)
            positive = jnp.sum(jnp.maximum(values, 0.0), axis=0, keepdims=True)
            part[slot, 0, b : b + 1, :] = positive[:, :SETS]
            part[slot, 1, b : b + 1, :] = positive[:, SETS:]

    me = j * 4 + c * 2 + p

    def final_copy(to):
        tj, tc, tp = lax.div(to, 4), lax.rem(lax.div(to, 2), 2), lax.rem(to, 2)
        return pltpu.make_async_remote_copy(
            src_ref=part.at[tj, tc], dst_ref=fin.at[me], send_sem=send_sem.at[4], recv_sem=recv_sem.at[4],
            device_id={"trade": tj * 4 + par * 2 + tc, "path": tp}, device_id_type=MESH,
        )

    def send_final(i, carry):
        final_copy(lax.rem(me + i, 16)).start()
        return carry

    lax.fori_loop(1, 16, send_final, 0)
    fin[me] = part[j, c]
    bytes_of(fin.at[pl.ds(0, 15)], recv_sem.at[4], False)
    out[...] = jnp.sum(fin[...], axis=0) * np.float32(1.0 / (ND * SLICE * 32))

    bytes_of(nt.at[pl.ds(0, ND - 1)], send_sem.at[0], True)
    bytes_of(cbuf.at[pl.ds(0, NJ - 1), c], send_sem.at[1], True)
    bytes_of(cbuf.at[:, c], send_sem.at[2], True)
    bytes_of(zbuf.at[pl.ds(0, 2 * ND - 1)], send_sem.at[3], True)
    bytes_of(fin.at[pl.ds(0, 15)], send_sem.at[4], True)


def shards(normals, chol, volatility, start_state, basis_map, basis_bias, coef, maturity, netting):
    args = (
        normals, chol, volatility.reshape(1, -1), start_state.reshape(1, -1), basis_map,
        basis_bias.reshape(1, -1), coef, maturity.reshape(1, -1), netting.reshape(1, -1),
    )
    return pl.pallas_call(
        kernel,
        out_shape=jax.ShapeDtypeStruct((NB, SETS), jnp.float32),
        in_specs=[pl.BlockSpec(memory_space=pl.ANY)] * len(args),
        out_specs=pl.BlockSpec(memory_space=pltpu.VMEM),
        scratch_shapes=[pltpu.VMEM(a.shape, a.dtype) for a in args]
        + [
            pltpu.VMEM((ND, SLICE, NB * F), jnp.bfloat16),
            pltpu.VMEM((ND, SLICE, NB * F), jnp.bfloat16),
            pltpu.VMEM((ND, SLICE, NB * F), jnp.bfloat16),
            pltpu.VMEM((2 * ND, SLICE, NB * F), jnp.bfloat16),
            pltpu.VMEM((NJ, 2, NB, 2 * K, SETS), jnp.bfloat16),
            pltpu.VMEM((2 * NB * F, NB * K), jnp.bfloat16),
            pltpu.VMEM((NJ, 2, NB, SETS), jnp.float32),
            pltpu.VMEM((16, NB, SETS), jnp.float32),
            pltpu.SemaphoreType.DMA((len(args),)),
            pltpu.SemaphoreType.DMA((5,)),
            pltpu.SemaphoreType.DMA((5,)),
            pltpu.SemaphoreType.DMA((NJ - 1,)),
        ],
        compiler_params=pltpu.CompilerParams(
            collective_id=0, has_side_effects=True, vmem_limit_bytes=32 << 20
        ),
    )(*args)


def solution(mesh):
    placed = (
        P("date", None, ("trade", "path")),
        P(),
        P(),
        P(),
        P(),
        P(),
        P(None, "trade"),
        P("trade"),
        P("trade"),
    )
    return jax.shard_map(
        shards, mesh=mesh, in_specs=placed, out_specs=P("date", "trade"), check_vma=False
    )
```

```python
import jax
import jax.numpy as jnp
import numpy as np
from jax import lax
from jax.experimental import pallas as pl
from jax.experimental.pallas import tpu as pltpu
from jax.sharding import PartitionSpec as P

MESH = pl.DeviceIdType.MESH
ND = 16
NB = 2
F = 64
K = 128
SETS = 128
SLICE = 16
NJ = 4
HIGH = lax.Precision.HIGHEST


def kernel(
    normals, chol, vol, start, bmap, bias, coef, mat, net,
    out,
    v_norm, v_chol, v_vol, v_start, v_bmap, v_bias, v_coef, v_mat, v_net,
    nt, arrived, sums, zbuf, cbuf, wbuf, part, fin,
    load_sem, send_sem, recv_sem, c_sem,
):
    d, t, p = lax.axis_index("date"), lax.axis_index("trade"), lax.axis_index("path")
    y, c = lax.div(t, 2), lax.rem(t, 2)
    j, par = lax.div(y, 2), lax.rem(y, 2)
    c1, p1 = 1 - c, 1 - p
    twin = t + 2 - 4 * par

    barrier = pltpu.get_barrier_semaphore()

    def hello(where):
        pl.semaphore_signal(barrier, inc=1, device_id=where, device_id_type=MESH)

    def hello_date(i, carry):
        hello({"date": lax.rem(d + i, ND)})
        return carry

    lax.fori_loop(1, ND, hello_date, 0)
    for i in range(1, NJ):
        hello({"trade": lax.rem(t + 4 * i, 16)})
    hello({"trade": twin})
    other = t + 1 - 2 * c
    hello({"trade": other})
    hello({"path": p1})
    hello({"trade": other, "path": p1})

    loads = [
        pltpu.make_async_copy(a, b, load_sem.at[i])
        for i, (a, b) in enumerate(
            (
                (normals, v_norm), (coef, v_coef), (mat, v_mat), (net, v_net), (chol, v_chol),
                (vol, v_vol), (start, v_start), (bmap, v_bmap), (bias, v_bias),
            )
        )
    ]
    for load in loads:
        load.start()

    loads[0].wait()
    flat = v_norm[...].reshape(NB * F, ND * SLICE).astype(jnp.float32)
    nt[...] = flat.T.astype(jnp.bfloat16).reshape(ND, SLICE, NB * F)
    arrived[d] = nt[d]

    for load in loads[1:4]:
        load.wait()
    local_set = v_net[...] - t * SETS
    trades = v_coef.shape[1]
    member = (lax.broadcasted_iota(jnp.int32, (SETS, trades), 0) == local_set)
    member = member.astype(jnp.float32).astype(jnp.bfloat16)
    for b in range(NB):
        alive = (d * NB + b < v_mat[...]).astype(jnp.float32).astype(jnp.bfloat16)
        folded = lax.dot_general(
            v_coef[...] * alive, member, (((1,), (1,)), ((), ())), preferred_element_type=jnp.float32
        )
        high = folded.astype(jnp.bfloat16)
        cbuf[j, c, b, :K, :] = high
        cbuf[j, c, b, K:, :] = (folded - high.astype(jnp.float32)).astype(jnp.bfloat16)

    pl.semaphore_wait(barrier, ND - 1 + NJ - 1 + 4)

    def slice_copy(e):
        return pltpu.make_async_remote_copy(
            src_ref=nt.at[e], dst_ref=arrived.at[d], send_sem=send_sem.at[0], recv_sem=recv_sem.at[0],
            device_id={"date": e}, device_id_type=MESH,
        )

    def send_slice(i, carry):
        slice_copy(lax.rem(d + i, ND)).start()
        return carry

    lax.fori_loop(1, ND, send_slice, 0)

    c_copies = [
        pltpu.make_async_remote_copy(
            src_ref=cbuf.at[j, c], dst_ref=cbuf.at[j, c], send_sem=send_sem.at[1], recv_sem=c_sem.at[i - 1],
            device_id={"trade": lax.rem(t + 4 * i, 16)}, device_id_type=MESH,
        )
        for i in range(1, NJ)
    ]
    for copy in c_copies:
        copy.start()

    def pass_on(slot):
        return pltpu.make_async_remote_copy(
            src_ref=cbuf.at[slot, c], dst_ref=cbuf.at[slot, c], send_sem=send_sem.at[2], recv_sem=recv_sem.at[2],
            device_id={"trade": other}, device_id_type=MESH,
        )

    pass_on(j).start()

    for load in loads[4:]:
        load.wait()
    scale = v_vol[...] * np.float32(np.sqrt(np.float32(1.0) / np.float32(ND * NB)))
    joint = jnp.dot(v_chol[...].T * scale, v_bmap[...], precision=HIGH, preferred_element_type=jnp.float32)
    offset = jnp.dot(v_start[...], v_bmap[...], precision=HIGH, preferred_element_type=jnp.float32) + v_bias[...]
    joint_high = joint.astype(jnp.bfloat16)
    joint_low = (joint - joint_high.astype(jnp.float32)).astype(jnp.bfloat16)
    wbuf[...] = jnp.zeros_like(wbuf)
    for b in range(NB):
        wbuf[pl.ds(b * F, F), pl.ds(b * K, K)] = joint_high
        wbuf[pl.ds(NB * F + b * F, F), pl.ds(b * K, K)] = joint_low
    offsets = jnp.concatenate([offset, offset], axis=1)

    def bytes_of(ref, sem, send):
        whole = pltpu.make_async_remote_copy(
            src_ref=ref, dst_ref=ref, send_sem=sem, recv_sem=sem, device_id={"trade": other}, device_id_type=MESH
        )
        return whole.wait_send() if send else whole.wait_recv()

    bytes_of(arrived.at[pl.ds(0, ND - 1)], recv_sem.at[0], False)
    later_half = lax.broadcasted_iota(jnp.int32, (SLICE, NB * F), 1) >= F
    total = jnp.zeros((SLICE, NB * F), jnp.float32)
    for e in range(ND):
        block = arrived[e].astype(jnp.float32)
        swapped = pltpu.roll(block, F, axis=1)
        pair = block + swapped
        sums[e] = (total + jnp.where(later_half, pair, block)).astype(jnp.bfloat16)
        total = total + pair

    def sums_copy(e, where):
        return pltpu.make_async_remote_copy(
            src_ref=sums.at[e], dst_ref=zbuf.at[par * ND + d], send_sem=send_sem.at[3], recv_sem=recv_sem.at[3],
            device_id={"date": e, "trade": where}, device_id_type=MESH,
        )

    def send_sums(i, carry):
        e = lax.rem(d + i, ND)
        sums_copy(e, t).start()
        sums_copy(e, twin).start()
        return carry

    lax.fori_loop(1, ND, send_sums, 0)
    sums_copy(d, twin).start()
    zbuf[par * ND + d] = sums[d]

    for i in range(1, NJ):
        c_copies[i - 1].wait_recv()
        pass_on(lax.rem(j + NJ - i, NJ)).start()

    bytes_of(zbuf.at[pl.ds(0, 2 * ND - 1)], recv_sem.at[3], False)
    z = zbuf[...].reshape(2 * ND * SLICE, NB * F)
    pre = jnp.dot(jnp.concatenate([z, z], axis=1), wbuf[...], preferred_element_type=jnp.float32)
    basis = jnp.tanh(pre + offsets).astype(jnp.bfloat16)

    bytes_of(cbuf.at[:, c1], recv_sem.at[2], False)
    for b in range(NB):
        own = basis[:, b * K : (b + 1) * K]
        twice = jnp.concatenate([own, own], axis=1)
        for slot in range(NJ):
            both = jnp.concatenate([cbuf[slot, 0, b], cbuf[slot, 1, b]], axis=1)
            values = jnp.dot(twice, both, preferred_element_type=jnp.float32)
            positive = jnp.sum(jnp.maximum(values, 0.0), axis=0, keepdims=True)
            part[slot, 0, b : b + 1, :] = positive[:, :SETS]
            part[slot, 1, b : b + 1, :] = positive[:, SETS:]

    me = j * 4 + c * 2 + p

    def final_copy(to):
        tj, tc, tp = lax.div(to, 4), lax.rem(lax.div(to, 2), 2), lax.rem(to, 2)
        return pltpu.make_async_remote_copy(
            src_ref=part.at[tj, tc], dst_ref=fin.at[me], send_sem=send_sem.at[4], recv_sem=recv_sem.at[4],
            device_id={"trade": tj * 4 + par * 2 + tc, "path": tp}, device_id_type=MESH,
        )

    def send_final(i, carry):
        final_copy(lax.rem(me + i, 16)).start()
        return carry

    lax.fori_loop(1, 16, send_final, 0)
    fin[me] = part[j, c]
    bytes_of(fin.at[pl.ds(0, 15)], recv_sem.at[4], False)
    out[...] = jnp.sum(fin[...], axis=0) * np.float32(1.0 / (ND * SLICE * 32))

    bytes_of(nt.at[pl.ds(0, ND - 1)], send_sem.at[0], True)
    bytes_of(cbuf.at[pl.ds(0, NJ - 1), c], send_sem.at[1], True)
    bytes_of(cbuf.at[:, c], send_sem.at[2], True)
    bytes_of(zbuf.at[pl.ds(0, 2 * ND - 1)], send_sem.at[3], True)
    bytes_of(fin.at[pl.ds(0, 15)], send_sem.at[4], True)


def shards(normals, chol, volatility, start_state, basis_map, basis_bias, coef, maturity, netting):
    args = (
        normals, chol, volatility.reshape(1, -1), start_state.reshape(1, -1), basis_map,
        basis_bias.reshape(1, -1), coef, maturity.reshape(1, -1), netting.reshape(1, -1),
    )
    return pl.pallas_call(
        kernel,
        out_shape=jax.ShapeDtypeStruct((NB, SETS), jnp.float32),
        in_specs=[pl.BlockSpec(memory_space=pltpu.HBM)] * len(args),
        out_specs=pl.BlockSpec(memory_space=pltpu.VMEM),
        scratch_shapes=[pltpu.VMEM(a.shape, a.dtype) for a in args]
        + [
            pltpu.VMEM((ND, SLICE, NB * F), jnp.bfloat16),
            pltpu.VMEM((ND, SLICE, NB * F), jnp.bfloat16),
            pltpu.VMEM((ND, SLICE, NB * F), jnp.bfloat16),
            pltpu.VMEM((2 * ND, SLICE, NB * F), jnp.bfloat16),
            pltpu.VMEM((NJ, 2, NB, 2 * K, SETS), jnp.bfloat16),
            pltpu.VMEM((2 * NB * F, NB * K), jnp.bfloat16),
            pltpu.VMEM((NJ, 2, NB, SETS), jnp.float32),
            pltpu.VMEM((16, NB, SETS), jnp.float32),
            pltpu.SemaphoreType.DMA((len(args),)),
            pltpu.SemaphoreType.DMA((5,)),
            pltpu.SemaphoreType.DMA((5,)),
            pltpu.SemaphoreType.DMA((NJ - 1,)),
        ],
        compiler_params=pltpu.CompilerParams(
            collective_id=0, has_side_effects=True, vmem_limit_bytes=60 << 20
        ),
    )(*args)


def solution(mesh):
    placed = (
        P("date", None, ("trade", "path")),
        P(),
        P(),
        P(),
        P(),
        P(),
        P(None, "trade"),
        P("trade"),
        P("trade"),
    )
    return jax.shard_map(
        shards, mesh=mesh, in_specs=placed, out_specs=P("date", "trade"), check_vma=False
    )
```

```python
import jax
import jax.numpy as jnp
import numpy as np
from jax import lax
from jax.experimental import pallas as pl
from jax.experimental.pallas import tpu as pltpu
from jax.sharding import PartitionSpec as P

MESH = pl.DeviceIdType.MESH
ND = 16
NB = 2
F = 64
K = 128
SETS = 128
NG = 4
GS = 4
SLICE = 64
NJ = 4
HIGH = lax.Precision.HIGHEST


def kernel(
    normals, chol, vol, start, bmap, bias, coef, mat, net,
    out,
    v_norm, v_chol, v_vol, v_start, v_bmap, v_bias, v_coef, v_mat, v_net,
    nt, arrived, tmsg, tbuf, sums, zbuf, cbuf, wbuf, part, fin,
    load_sem, send_sem, recv_sem, c_sem, t_sem, t_sent, ready,
):
    d, t, p = lax.axis_index("date"), lax.axis_index("trade"), lax.axis_index("path")
    y, c = lax.div(t, 2), lax.rem(t, 2)
    j, par = lax.div(y, 2), lax.rem(y, 2)
    g, w = lax.div(d, GS), lax.rem(d, GS)
    c1, p1 = 1 - c, 1 - p
    twin = t + 2 - 4 * par

    barrier = pltpu.get_barrier_semaphore()

    def hello(where):
        pl.semaphore_signal(barrier, inc=1, device_id=where, device_id_type=MESH)

    def mate(i):
        return g * GS + lax.rem(w + i, GS)

    def later_group(i):
        return i * GS + w

    for i in range(1, GS):
        hello({"date": mate(i)})
    for i in range(1, NJ):
        hello({"trade": lax.rem(t + 4 * i, 16)})
    hello({"trade": twin})
    other = t + 1 - 2 * c
    hello({"trade": other})
    hello({"path": p1})
    hello({"trade": other, "path": p1})

    def hello_later(i, carry):
        hello({"date": later_group(i)})
        return carry

    lax.fori_loop(g + 1, NG, hello_later, 0)

    loads = [
        pltpu.make_async_copy(a, b, load_sem.at[i])
        for i, (a, b) in enumerate(
            (
                (normals, v_norm), (coef, v_coef), (mat, v_mat), (net, v_net), (chol, v_chol),
                (vol, v_vol), (start, v_start), (bmap, v_bmap), (bias, v_bias),
            )
        )
    ]
    for load in loads:
        load.start()

    loads[0].wait()
    flat = v_norm[...].reshape(NB * F, GS * SLICE).astype(jnp.float32)
    nt[...] = flat.T.astype(jnp.bfloat16).reshape(GS, SLICE, NB * F)
    arrived[w] = nt[w]

    for load in loads[1:4]:
        load.wait()
    local_set = v_net[...] - t * SETS
    trades = v_coef.shape[1]
    member = (lax.broadcasted_iota(jnp.int32, (SETS, trades), 0) == local_set)
    member = member.astype(jnp.float32).astype(jnp.bfloat16)
    for b in range(NB):
        alive = (d * NB + b < v_mat[...]).astype(jnp.float32).astype(jnp.bfloat16)
        folded = lax.dot_general(
            v_coef[...] * alive, member, (((1,), (1,)), ((), ())), preferred_element_type=jnp.float32
        )
        high = folded.astype(jnp.bfloat16)
        cbuf[j, c, b, :K, :] = high
        cbuf[j, c, b, K:, :] = (folded - high.astype(jnp.float32)).astype(jnp.bfloat16)

    pl.semaphore_wait(barrier, GS - 1 + g + NJ - 1 + 4)

    for i in range(1, GS):
        pltpu.make_async_remote_copy(
            src_ref=nt.at[lax.rem(w + i, GS)], dst_ref=arrived.at[w], send_sem=send_sem.at[0], recv_sem=recv_sem.at[0],
            device_id={"date": mate(i)}, device_id_type=MESH,
        ).start()

    def say_ready(i, carry):
        pl.semaphore_signal(ready.at[g], inc=1, device_id={"date": later_group(i)}, device_id_type=MESH)
        return carry

    lax.fori_loop(0, g, say_ready, 0)

    c_copies = [
        pltpu.make_async_remote_copy(
            src_ref=cbuf.at[j, c], dst_ref=cbuf.at[j, c], send_sem=send_sem.at[1], recv_sem=c_sem.at[i - 1],
            device_id={"trade": lax.rem(t + 4 * i, 16)}, device_id_type=MESH,
        )
        for i in range(1, NJ)
    ]
    for copy in c_copies:
        copy.start()

    def pass_on(slot):
        return pltpu.make_async_remote_copy(
            src_ref=cbuf.at[slot, c], dst_ref=cbuf.at[slot, c], send_sem=send_sem.at[2], recv_sem=recv_sem.at[2],
            device_id={"trade": other}, device_id_type=MESH,
        )

    pass_on(j).start()

    for load in loads[4:]:
        load.wait()
    scale = v_vol[...] * np.float32(np.sqrt(np.float32(1.0) / np.float32(ND * NB)))
    joint = jnp.dot(v_chol[...].T * scale, v_bmap[...], precision=HIGH, preferred_element_type=jnp.float32)
    offset = jnp.dot(v_start[...], v_bmap[...], precision=HIGH, preferred_element_type=jnp.float32) + v_bias[...]
    joint_high = joint.astype(jnp.bfloat16)
    joint_low = (joint - joint_high.astype(jnp.float32)).astype(jnp.bfloat16)
    wbuf[...] = jnp.zeros_like(wbuf)
    for b in range(NB):
        wbuf[pl.ds(b * F, F), pl.ds(b * K, K)] = joint_high
        wbuf[pl.ds(NB * F + b * F, F), pl.ds(b * K, K)] = joint_low
    offsets = jnp.concatenate([offset, offset], axis=1)

    def bytes_of(ref, sem, send):
        whole = pltpu.make_async_remote_copy(
            src_ref=ref, dst_ref=ref, send_sem=sem, recv_sem=sem, device_id={"trade": other}, device_id_type=MESH
        )
        return whole.wait_send() if send else whole.wait_recv()

    bytes_of(arrived.at[pl.ds(0, GS - 1)], recv_sem.at[0], False)
    later_half = lax.broadcasted_iota(jnp.int32, (SLICE, NB * F), 1) >= F
    total = jnp.zeros((SLICE, NB * F), jnp.float32)
    for e in range(GS):
        block = arrived[e].astype(jnp.float32)
        total = total + (block + pltpu.roll(block, F, axis=1))
    total_high = total.astype(jnp.bfloat16)
    tmsg[...] = jnp.where(later_half, total - total_high.astype(jnp.float32), total).astype(jnp.bfloat16)

    def earlier(i, carry):
        pltpu.make_async_remote_copy(
            src_ref=tmsg, dst_ref=tbuf.at[i], send_sem=t_sent.at[i], recv_sem=t_sem.at[i],
            device_id={"trade": other}, device_id_type=MESH,
        ).wait_recv()
        both = tbuf[i].astype(jnp.float32)
        return carry + (both + pltpu.roll(both, F, axis=1))

    total = lax.fori_loop(0, g, earlier, jnp.zeros((SLICE, NB * F), jnp.float32))
    for e in range(GS):
        block = arrived[e].astype(jnp.float32)
        pair = block + pltpu.roll(block, F, axis=1)
        sums[e] = (total + jnp.where(later_half, pair, block)).astype(jnp.bfloat16)
        total = total + pair

    def sums_copy(e, where):
        return pltpu.make_async_remote_copy(
            src_ref=sums.at[e], dst_ref=zbuf.at[par * GS + w], send_sem=send_sem.at[3], recv_sem=recv_sem.at[3],
            device_id={"date": g * GS + e, "trade": where}, device_id_type=MESH,
        )

    for i in range(1, GS):
        e = lax.rem(w + i, GS)
        sums_copy(e, twin).start()
        sums_copy(e, t).start()
    sums_copy(w, twin).start()
    zbuf[par * GS + w] = sums[w]

    def total_copy(i):
        return pltpu.make_async_remote_copy(
            src_ref=tmsg, dst_ref=tbuf.at[g], send_sem=t_sent.at[i], recv_sem=t_sem.at[g],
            device_id={"date": later_group(i)}, device_id_type=MESH,
        )

    def send_total(i, carry):
        pl.semaphore_wait(ready.at[i], 1)
        total_copy(i).start()
        return carry

    lax.fori_loop(g + 1, NG, send_total, 0)

    for i in range(1, NJ):
        c_copies[i - 1].wait_recv()
        pass_on(lax.rem(j + NJ - i, NJ)).start()

    bytes_of(zbuf.at[pl.ds(0, 2 * GS - 1)], recv_sem.at[3], False)
    z = zbuf[...].reshape(2 * GS * SLICE, NB * F)
    pre = jnp.dot(jnp.concatenate([z, z], axis=1), wbuf[...], preferred_element_type=jnp.float32)
    basis = jnp.tanh(pre + offsets).astype(jnp.bfloat16)

    bytes_of(cbuf.at[:, c1], recv_sem.at[2], False)
    for b in range(NB):
        own = basis[:, b * K : (b + 1) * K]
        twice = jnp.concatenate([own, own], axis=1)
        for slot in range(NJ):
            both = jnp.concatenate([cbuf[slot, 0, b], cbuf[slot, 1, b]], axis=1)
            values = jnp.dot(twice, both, preferred_element_type=jnp.float32)
            positive = jnp.sum(jnp.maximum(values, 0.0), axis=0, keepdims=True)
            part[slot, 0, b : b + 1, :] = positive[:, :SETS]
            part[slot, 1, b : b + 1, :] = positive[:, SETS:]

    me = j * 4 + c * 2 + p

    def final_copy(to):
        tj, tc, tp = lax.div(to, 4), lax.rem(lax.div(to, 2), 2), lax.rem(to, 2)
        return pltpu.make_async_remote_copy(
            src_ref=part.at[tj, tc], dst_ref=fin.at[me], send_sem=send_sem.at[4], recv_sem=recv_sem.at[4],
            device_id={"trade": tj * 4 + par * 2 + tc, "path": tp}, device_id_type=MESH,
        )

    def send_final(i, carry):
        final_copy(lax.rem(me + i, 16)).start()
        return carry

    lax.fori_loop(1, 16, send_final, 0)
    fin[me] = part[j, c]
    bytes_of(fin.at[pl.ds(0, 15)], recv_sem.at[4], False)
    out[...] = jnp.sum(fin[...], axis=0) * np.float32(1.0 / (GS * SLICE * 32))

    bytes_of(nt.at[pl.ds(0, GS - 1)], send_sem.at[0], True)
    bytes_of(cbuf.at[pl.ds(0, NJ - 1), c], send_sem.at[1], True)
    bytes_of(cbuf.at[:, c], send_sem.at[2], True)
    bytes_of(zbuf.at[pl.ds(0, 2 * GS - 1)], send_sem.at[3], True)
    bytes_of(fin.at[pl.ds(0, 15)], send_sem.at[4], True)

    def sent_total(i, carry):
        total_copy(i).wait_send()
        return carry

    lax.fori_loop(g + 1, NG, sent_total, 0)


def shards(normals, chol, volatility, start_state, basis_map, basis_bias, coef, maturity, netting):
    args = (
        normals, chol, volatility.reshape(1, -1), start_state.reshape(1, -1), basis_map,
        basis_bias.reshape(1, -1), coef, maturity.reshape(1, -1), netting.reshape(1, -1),
    )
    return pl.pallas_call(
        kernel,
        out_shape=jax.ShapeDtypeStruct((NB, SETS), jnp.float32),
        in_specs=[pl.BlockSpec(memory_space=pltpu.HBM)] * len(args),
        out_specs=pl.BlockSpec(memory_space=pltpu.VMEM),
        scratch_shapes=[pltpu.VMEM(a.shape, a.dtype) for a in args]
        + [
            pltpu.VMEM((GS, SLICE, NB * F), jnp.bfloat16),
            pltpu.VMEM((GS, SLICE, NB * F), jnp.bfloat16),
            pltpu.VMEM((SLICE, NB * F), jnp.bfloat16),
            pltpu.VMEM((NG - 1, SLICE, NB * F), jnp.bfloat16),
            pltpu.VMEM((GS, SLICE, NB * F), jnp.bfloat16),
            pltpu.VMEM((2 * GS, SLICE, NB * F), jnp.bfloat16),
            pltpu.VMEM((NJ, 2, NB, 2 * K, SETS), jnp.bfloat16),
            pltpu.VMEM((2 * NB * F, NB * K), jnp.bfloat16),
            pltpu.VMEM((NJ, 2, NB, SETS), jnp.float32),
            pltpu.VMEM((16, NB, SETS), jnp.float32),
            pltpu.SemaphoreType.DMA((len(args),)),
            pltpu.SemaphoreType.DMA((5,)),
            pltpu.SemaphoreType.DMA((5,)),
            pltpu.SemaphoreType.DMA((NJ - 1,)),
            pltpu.SemaphoreType.DMA((NG - 1,)),
            pltpu.SemaphoreType.DMA((NG,)),
            pltpu.SemaphoreType.REGULAR((NG,)),
        ],
        compiler_params=pltpu.CompilerParams(
            collective_id=0, has_side_effects=True, vmem_limit_bytes=60 << 20
        ),
    )(*args)


def solution(mesh):
    placed = (
        P("date", None, ("trade", "path")),
        P(),
        P(),
        P(),
        P(),
        P(),
        P(None, "trade"),
        P("trade"),
        P("trade"),
    )
    return jax.shard_map(
        shards, mesh=mesh, in_specs=placed, out_specs=P("date", "trade"), check_vma=False
    )
```

```python
import jax
import jax.numpy as jnp
import numpy as np
from jax import lax
from jax.experimental import pallas as pl
from jax.experimental.pallas import tpu as pltpu
from jax.sharding import PartitionSpec as P

MESH = pl.DeviceIdType.MESH
ND = 16
NB = 2
F = 64
K = 128
SETS = 128
NG = 4
GS = 4
SLICE = 64
TOP = 127 * 256
NJ = 4
HIGH = lax.Precision.HIGHEST


def kernel(
    normals, chol, vol, start, bmap, bias, coef, mat, net,
    out,
    v_norm, v_chol, v_vol, v_start, v_bmap, v_bias, v_coef, v_mat, v_net,
    nt, arrived, tmsg, tbuf, sums, zbuf, cbuf, cwide, unit, wbuf, part, fin,
    load_sem, send_sem, recv_sem, c_sem, t_sem, t_sent, ready,
):
    d, t, p = lax.axis_index("date"), lax.axis_index("trade"), lax.axis_index("path")
    y, c = lax.div(t, 2), lax.rem(t, 2)
    j, par = lax.div(y, 2), lax.rem(y, 2)
    g, w = lax.div(d, GS), lax.rem(d, GS)
    c1, p1 = 1 - c, 1 - p
    twin = t + 2 - 4 * par

    barrier = pltpu.get_barrier_semaphore()

    def hello(where):
        pl.semaphore_signal(barrier, inc=1, device_id=where, device_id_type=MESH)

    def mate(i):
        return g * GS + lax.rem(w + i, GS)

    def later_group(i):
        return i * GS + w

    for i in range(1, GS):
        hello({"date": mate(i)})
    for i in range(1, NJ):
        hello({"trade": lax.rem(t + 4 * i, 16)})
    hello({"trade": twin})
    other = t + 1 - 2 * c
    hello({"trade": other})
    hello({"path": p1})
    hello({"trade": other, "path": p1})

    def hello_later(i, carry):
        hello({"date": later_group(i)})
        return carry

    lax.fori_loop(g + 1, NG, hello_later, 0)

    loads = [
        pltpu.make_async_copy(a, b, load_sem.at[i])
        for i, (a, b) in enumerate(
            (
                (normals, v_norm), (coef, v_coef), (mat, v_mat), (net, v_net), (chol, v_chol),
                (vol, v_vol), (start, v_start), (bmap, v_bmap), (bias, v_bias),
            )
        )
    ]
    for load in loads:
        load.start()

    loads[0].wait()
    flat = v_norm[...].reshape(NB * F, GS * SLICE).astype(jnp.float32)
    nt[...] = flat.T.astype(jnp.bfloat16).reshape(GS, SLICE, NB * F)
    arrived[w] = nt[w]

    for load in loads[1:4]:
        load.wait()
    local_set = v_net[...] - t * SETS
    trades = v_coef.shape[1]
    member = (lax.broadcasted_iota(jnp.int32, (SETS, trades), 0) == local_set)
    member = member.astype(jnp.float32).astype(jnp.bfloat16)
    for b in range(NB):
        alive = (d * NB + b < v_mat[...]).astype(jnp.float32).astype(jnp.bfloat16)
        folded = lax.dot_general(
            v_coef[...] * alive, member, (((1,), (1,)), ((), ())), preferred_element_type=jnp.float32
        )
        largest = jnp.maximum(jnp.max(jnp.abs(folded), axis=0, keepdims=True), np.float32(1e-30))
        unit[b : b + 1, :] = largest * np.float32(1.0 / TOP)
        cbuf[j, c, b] = jnp.round(folded * (np.float32(TOP) / largest)).astype(jnp.int32).astype(jnp.int16)

    pl.semaphore_wait(barrier, GS - 1 + g + NJ - 1 + 4)

    for i in range(1, GS):
        pltpu.make_async_remote_copy(
            src_ref=nt.at[lax.rem(w + i, GS)], dst_ref=arrived.at[w], send_sem=send_sem.at[0], recv_sem=recv_sem.at[0],
            device_id={"date": mate(i)}, device_id_type=MESH,
        ).start()

    def say_ready(i, carry):
        pl.semaphore_signal(ready.at[g], inc=1, device_id={"date": later_group(i)}, device_id_type=MESH)
        return carry

    lax.fori_loop(0, g, say_ready, 0)

    c_copies = [
        pltpu.make_async_remote_copy(
            src_ref=cbuf.at[j, c], dst_ref=cbuf.at[j, c], send_sem=send_sem.at[1], recv_sem=c_sem.at[i - 1],
            device_id={"trade": lax.rem(t + 4 * i, 16)}, device_id_type=MESH,
        )
        for i in range(1, NJ)
    ]
    for copy in c_copies:
        copy.start()

    def pass_on(slot):
        return pltpu.make_async_remote_copy(
            src_ref=cbuf.at[slot, c], dst_ref=cbuf.at[slot, c], send_sem=send_sem.at[2], recv_sem=recv_sem.at[2],
            device_id={"trade": other}, device_id_type=MESH,
        )

    pass_on(j).start()

    for load in loads[4:]:
        load.wait()
    scale = v_vol[...] * np.float32(np.sqrt(np.float32(1.0) / np.float32(ND * NB)))
    joint = jnp.dot(v_chol[...].T * scale, v_bmap[...], precision=HIGH, preferred_element_type=jnp.float32)
    offset = jnp.dot(v_start[...], v_bmap[...], precision=HIGH, preferred_element_type=jnp.float32) + v_bias[...]
    joint_high = joint.astype(jnp.bfloat16)
    joint_low = (joint - joint_high.astype(jnp.float32)).astype(jnp.bfloat16)
    wbuf[...] = jnp.zeros_like(wbuf)
    for b in range(NB):
        wbuf[pl.ds(b * F, F), pl.ds(b * K, K)] = joint_high
        wbuf[pl.ds(NB * F + b * F, F), pl.ds(b * K, K)] = joint_low
    offsets = jnp.concatenate([offset, offset], axis=1)

    def bytes_of(ref, sem, send):
        whole = pltpu.make_async_remote_copy(
            src_ref=ref, dst_ref=ref, send_sem=sem, recv_sem=sem, device_id={"trade": other}, device_id_type=MESH
        )
        return whole.wait_send() if send else whole.wait_recv()

    bytes_of(arrived.at[pl.ds(0, GS - 1)], recv_sem.at[0], False)
    later_half = lax.broadcasted_iota(jnp.int32, (SLICE, NB * F), 1) >= F
    total = jnp.zeros((SLICE, NB * F), jnp.float32)
    for e in range(GS):
        block = arrived[e].astype(jnp.float32)
        total = total + (block + pltpu.roll(block, F, axis=1))
    total_high = total.astype(jnp.bfloat16)
    tmsg[...] = jnp.where(later_half, total - total_high.astype(jnp.float32), total).astype(jnp.bfloat16)

    def earlier(i, carry):
        pltpu.make_async_remote_copy(
            src_ref=tmsg, dst_ref=tbuf.at[i], send_sem=t_sent.at[i], recv_sem=t_sem.at[i],
            device_id={"trade": other}, device_id_type=MESH,
        ).wait_recv()
        both = tbuf[i].astype(jnp.float32)
        return carry + (both + pltpu.roll(both, F, axis=1))

    total = lax.fori_loop(0, g, earlier, jnp.zeros((SLICE, NB * F), jnp.float32))
    for e in range(GS):
        block = arrived[e].astype(jnp.float32)
        pair = block + pltpu.roll(block, F, axis=1)
        sums[e] = (total + jnp.where(later_half, pair, block)).astype(jnp.bfloat16)
        total = total + pair

    def sums_copy(e, where):
        return pltpu.make_async_remote_copy(
            src_ref=sums.at[e], dst_ref=zbuf.at[par * GS + w], send_sem=send_sem.at[3], recv_sem=recv_sem.at[3],
            device_id={"date": g * GS + e, "trade": where}, device_id_type=MESH,
        )

    for i in range(1, GS):
        e = lax.rem(w + i, GS)
        sums_copy(e, twin).start()
        sums_copy(e, t).start()
    sums_copy(w, twin).start()
    zbuf[par * GS + w] = sums[w]

    def total_copy(i):
        return pltpu.make_async_remote_copy(
            src_ref=tmsg, dst_ref=tbuf.at[g], send_sem=t_sent.at[i], recv_sem=t_sem.at[g],
            device_id={"date": later_group(i)}, device_id_type=MESH,
        )

    def send_total(i, carry):
        pl.semaphore_wait(ready.at[i], 1)
        total_copy(i).start()
        return carry

    lax.fori_loop(g + 1, NG, send_total, 0)

    def widen(slot, core):
        for b in range(NB):
            whole = cbuf[slot, core, b].astype(jnp.int32).astype(jnp.float32)
            coarse = jnp.round(whole * np.float32(1 / 256)) * np.float32(256)
            cwide[slot, core, b, :K, :] = coarse.astype(jnp.bfloat16)
            cwide[slot, core, b, K:, :] = (whole - coarse).astype(jnp.bfloat16)

    widen(j, c)
    for i in range(1, NJ):
        slot = lax.rem(j + NJ - i, NJ)
        c_copies[i - 1].wait_recv()
        pass_on(slot).start()
        widen(slot, c)
    bytes_of(cbuf.at[:, c1], recv_sem.at[2], False)
    for slot in range(NJ):
        widen(slot, c1)

    bytes_of(zbuf.at[pl.ds(0, 2 * GS - 1)], recv_sem.at[3], False)
    z = zbuf[...].reshape(2 * GS * SLICE, NB * F)
    pre = jnp.dot(jnp.concatenate([z, z], axis=1), wbuf[...], preferred_element_type=jnp.float32)
    basis = jnp.tanh(pre + offsets).astype(jnp.bfloat16)
    twice = [jnp.concatenate([basis[:, b * K : (b + 1) * K]] * 2, axis=1) for b in range(NB)]

    def final_copy(slot, tc, tp):
        return pltpu.make_async_remote_copy(
            src_ref=part.at[slot, tc], dst_ref=fin.at[j * 4 + c * 2 + p], send_sem=send_sem.at[4], recv_sem=recv_sem.at[4],
            device_id={"trade": slot * 4 + par * 2 + tc, "path": tp}, device_id_type=MESH,
        )

    for i in (2, 1, 3, 0):
        slot = lax.rem(j + i, NJ)
        for b in range(NB):
            both = jnp.concatenate([cwide[slot, 0, b], cwide[slot, 1, b]], axis=1)
            values = jnp.dot(twice[b], both, preferred_element_type=jnp.float32)
            positive = jnp.sum(jnp.maximum(values, 0.0), axis=0, keepdims=True)
            part[slot, 0, b : b + 1, :] = positive[:, :SETS]
            part[slot, 1, b : b + 1, :] = positive[:, SETS:]
        final_copy(slot, c, p1).start()
        final_copy(slot, c1, p1).start()
        final_copy(slot, c1, p).start()
        if i:
            final_copy(slot, c, p).start()

    fin[j * 4 + c * 2 + p] = part[j, c]
    bytes_of(fin.at[pl.ds(0, 15)], recv_sem.at[4], False)
    out[...] = jnp.sum(fin[...], axis=0) * unit[...] * np.float32(1.0 / (GS * SLICE * 32))

    bytes_of(nt.at[pl.ds(0, GS - 1)], send_sem.at[0], True)
    bytes_of(cbuf.at[pl.ds(0, NJ - 1), c], send_sem.at[1], True)
    bytes_of(cbuf.at[:, c], send_sem.at[2], True)
    bytes_of(zbuf.at[pl.ds(0, 2 * GS - 1)], send_sem.at[3], True)
    bytes_of(fin.at[pl.ds(0, 15)], send_sem.at[4], True)

    def sent_total(i, carry):
        total_copy(i).wait_send()
        return carry

    lax.fori_loop(g + 1, NG, sent_total, 0)


def shards(normals, chol, volatility, start_state, basis_map, basis_bias, coef, maturity, netting):
    args = (
        normals, chol, volatility.reshape(1, -1), start_state.reshape(1, -1), basis_map,
        basis_bias.reshape(1, -1), coef, maturity.reshape(1, -1), netting.reshape(1, -1),
    )
    return pl.pallas_call(
        kernel,
        out_shape=jax.ShapeDtypeStruct((NB, SETS), jnp.float32),
        in_specs=[pl.BlockSpec(memory_space=pltpu.HBM)] * len(args),
        out_specs=pl.BlockSpec(memory_space=pltpu.VMEM),
        scratch_shapes=[pltpu.VMEM(a.shape, a.dtype) for a in args]
        + [
            pltpu.VMEM((GS, SLICE, NB * F), jnp.bfloat16),
            pltpu.VMEM((GS, SLICE, NB * F), jnp.bfloat16),
            pltpu.VMEM((SLICE, NB * F), jnp.bfloat16),
            pltpu.VMEM((NG - 1, SLICE, NB * F), jnp.bfloat16),
            pltpu.VMEM((GS, SLICE, NB * F), jnp.bfloat16),
            pltpu.VMEM((2 * GS, SLICE, NB * F), jnp.bfloat16),
            pltpu.VMEM((NJ, 2, NB, K, SETS), jnp.int16),
            pltpu.VMEM((NJ, 2, NB, 2 * K, SETS), jnp.bfloat16),
            pltpu.VMEM((NB, SETS), jnp.float32),
            pltpu.VMEM((2 * NB * F, NB * K), jnp.bfloat16),
            pltpu.VMEM((NJ, 2, NB, SETS), jnp.float32),
            pltpu.VMEM((16, NB, SETS), jnp.float32),
            pltpu.SemaphoreType.DMA((len(args),)),
            pltpu.SemaphoreType.DMA((5,)),
            pltpu.SemaphoreType.DMA((5,)),
            pltpu.SemaphoreType.DMA((NJ - 1,)),
            pltpu.SemaphoreType.DMA((NG - 1,)),
            pltpu.SemaphoreType.DMA((NG,)),
            pltpu.SemaphoreType.REGULAR((NG,)),
        ],
        compiler_params=pltpu.CompilerParams(
            collective_id=0, has_side_effects=True, vmem_limit_bytes=60 << 20
        ),
    )(*args)


def solution(mesh):
    placed = (
        P("date", None, ("trade", "path")),
        P(),
        P(),
        P(),
        P(),
        P(),
        P(None, "trade"),
        P("trade"),
        P("trade"),
    )
    return jax.shard_map(
        shards, mesh=mesh, in_specs=placed, out_specs=P("date", "trade"), check_vma=False
    )
```

```python
import jax
import jax.numpy as jnp
import numpy as np
from jax import lax
from jax.experimental import pallas as pl
from jax.experimental.pallas import tpu as pltpu
from jax.sharding import PartitionSpec as P

MESH = pl.DeviceIdType.MESH
ND = 16
NB = 2
F = 64
K = 128
SETS = 128
GS = 4
SLICE = 64
TOP = 127 * 256
NJ = 4
HIGH = lax.Precision.HIGHEST


def kernel(
    normals, chol, vol, start, bmap, bias, coef, mat, net,
    out,
    v_norm, v_chol, v_vol, v_start, v_bmap, v_bias, v_coef, v_mat, v_net,
    nt, arrived, ahead, tmsg, tbuf, base, sums, zbuf, cbuf, cwide, unit, wbuf, part, fin,
    load_sem, send_sem, recv_sem, c_sem, t_sem, t_sent, ready,
):
    d, t, p = lax.axis_index("date"), lax.axis_index("trade"), lax.axis_index("path")
    y, c = lax.div(t, 2), lax.rem(t, 2)
    j, par = lax.div(y, 2), lax.rem(y, 2)
    g, w = lax.div(d, GS), lax.rem(d, GS)
    c1, p1 = 1 - c, 1 - p
    twin = t + 2 - 4 * par

    barrier = pltpu.get_barrier_semaphore()

    def hello(where):
        pl.semaphore_signal(barrier, inc=1, device_id=where, device_id_type=MESH)

    def mate(i):
        return g * GS + lax.rem(w + i, GS)

    def counterpart(group):
        return {"date": group * GS + w}

    for i in range(1, GS):
        hello({"date": mate(i)})
    for i in range(1, NJ):
        hello({"trade": lax.rem(t + 4 * i, 16)})
    hello({"trade": twin})
    other = t + 1 - 2 * c
    hello({"trade": other})
    hello({"path": p1})
    hello({"trade": other, "path": p1})

    @pl.when(g == 0)
    def _():
        hello(counterpart(1))
        hello(counterpart(3))

    @pl.when(g == 1)
    def _():
        hello(counterpart(2))

    @pl.when(g == 3)
    def _():
        for i in range(GS):
            hello({"date": 2 * GS + i})

    loads = [
        pltpu.make_async_copy(a, b, load_sem.at[i])
        for i, (a, b) in enumerate(
            (
                (normals, v_norm), (coef, v_coef), (mat, v_mat), (net, v_net), (chol, v_chol),
                (vol, v_vol), (start, v_start), (bmap, v_bmap), (bias, v_bias),
            )
        )
    ]
    for load in loads:
        load.start()

    loads[0].wait()
    flat = v_norm[...].reshape(NB * F, GS * SLICE).astype(jnp.float32)
    nt[...] = flat.T.astype(jnp.bfloat16).reshape(GS, SLICE, NB * F)
    arrived[w] = nt[w]

    for load in loads[1:4]:
        load.wait()
    local_set = v_net[...] - t * SETS
    trades = v_coef.shape[1]
    member = (lax.broadcasted_iota(jnp.int32, (SETS, trades), 0) == local_set)
    member = member.astype(jnp.float32).astype(jnp.bfloat16)
    for b in range(NB):
        alive = (d * NB + b < v_mat[...]).astype(jnp.float32).astype(jnp.bfloat16)
        folded = lax.dot_general(
            v_coef[...] * alive, member, (((1,), (1,)), ((), ())), preferred_element_type=jnp.float32
        )
        largest = jnp.maximum(jnp.max(jnp.abs(folded), axis=0, keepdims=True), np.float32(1e-30))
        unit[b : b + 1, :] = largest * np.float32(1.0 / TOP)
        cbuf[j, c, b] = jnp.round(folded * (np.float32(TOP) / largest)).astype(jnp.int32).astype(jnp.int16)

    heard = jnp.where(g == 0, 0, 1) + jnp.where(g == 2, GS, 0)
    pl.semaphore_wait(barrier, GS - 1 + NJ - 1 + 4 + heard)

    for i in range(1, GS):
        pltpu.make_async_remote_copy(
            src_ref=nt.at[lax.rem(w + i, GS)], dst_ref=arrived.at[w], send_sem=send_sem.at[0], recv_sem=recv_sem.at[0],
            device_id={"date": mate(i)}, device_id_type=MESH,
        ).start()

    @pl.when(g == 2)
    def _():
        for i in range(GS):
            pltpu.make_async_remote_copy(
                src_ref=nt.at[i], dst_ref=ahead.at[w], send_sem=send_sem.at[5], recv_sem=recv_sem.at[5],
                device_id={"date": 3 * GS + i}, device_id_type=MESH,
            ).start()

    def say_ready(to, slot):
        pl.semaphore_signal(ready.at[slot], inc=1, device_id=counterpart(to), device_id_type=MESH)

    @pl.when(g == 1)
    def _():
        say_ready(0, 0)

    @pl.when(g == 2)
    def _():
        say_ready(1, 0)

    @pl.when(g == 3)
    def _():
        say_ready(0, 1)

    c_copies = [
        pltpu.make_async_remote_copy(
            src_ref=cbuf.at[j, c], dst_ref=cbuf.at[j, c], send_sem=send_sem.at[1], recv_sem=c_sem.at[i - 1],
            device_id={"trade": lax.rem(t + 4 * i, 16)}, device_id_type=MESH,
        )
        for i in range(1, NJ)
    ]
    for copy in c_copies:
        copy.start()

    def pass_on(slot):
        return pltpu.make_async_remote_copy(
            src_ref=cbuf.at[slot, c], dst_ref=cbuf.at[slot, c], send_sem=send_sem.at[2], recv_sem=recv_sem.at[2],
            device_id={"trade": other}, device_id_type=MESH,
        )

    pass_on(j).start()

    for load in loads[4:]:
        load.wait()
    scale = v_vol[...] * np.float32(np.sqrt(np.float32(1.0) / np.float32(ND * NB)))
    joint = jnp.dot(v_chol[...].T * scale, v_bmap[...], precision=HIGH, preferred_element_type=jnp.float32)
    offset = jnp.dot(v_start[...], v_bmap[...], precision=HIGH, preferred_element_type=jnp.float32) + v_bias[...]
    joint_high = joint.astype(jnp.bfloat16)
    joint_low = (joint - joint_high.astype(jnp.float32)).astype(jnp.bfloat16)
    wbuf[...] = jnp.zeros_like(wbuf)
    for b in range(NB):
        wbuf[pl.ds(b * F, F), pl.ds(b * K, K)] = joint_high
        wbuf[pl.ds(NB * F + b * F, F), pl.ds(b * K, K)] = joint_low
    offsets = jnp.concatenate([offset, offset], axis=1)

    def bytes_of(ref, sem, send):
        whole = pltpu.make_async_remote_copy(
            src_ref=ref, dst_ref=ref, send_sem=sem, recv_sem=sem, device_id={"trade": other}, device_id_type=MESH
        )
        return whole.wait_send() if send else whole.wait_recv()

    bytes_of(arrived.at[pl.ds(0, GS - 1)], recv_sem.at[0], False)
    later_half = lax.broadcasted_iota(jnp.int32, (SLICE, NB * F), 1) >= F

    def twofold(message):
        message = message.astype(jnp.float32)
        return message + pltpu.roll(message, F, axis=1)

    def terms(value):
        high = value.astype(jnp.bfloat16).astype(jnp.float32)
        return jnp.where(later_half, value - high, value).astype(jnp.bfloat16)

    own = sum(twofold(arrived[e]) for e in range(GS))
    tmsg[0] = terms(own)

    def total_copy(to, message, slot):
        return pltpu.make_async_remote_copy(
            src_ref=tmsg.at[message], dst_ref=tbuf.at[slot], send_sem=t_sent.at[message], recv_sem=t_sem.at[slot],
            device_id=counterpart(to), device_id_type=MESH,
        )

    @pl.when(g == 0)
    def _():
        base[...] = jnp.zeros_like(base)

    @pl.when(g == 1)
    def _():
        total_copy(0, 0, 1).start()

    @pl.when(g > 0)
    def _():
        total_copy(0, 0, 0).wait_recv()
        base[...] = twofold(tbuf[0])

    @pl.when(g == 3)
    def _():
        bytes_of(ahead, recv_sem.at[5], False)
        base[...] += sum(twofold(ahead[e]) for e in range(GS))

    total = base[...]
    for e in range(GS):
        block = arrived[e].astype(jnp.float32)
        pair = block + pltpu.roll(block, F, axis=1)
        sums[e] = (total + jnp.where(later_half, pair, block)).astype(jnp.bfloat16)
        total = total + pair

    def sums_copy(e, where):
        return pltpu.make_async_remote_copy(
            src_ref=sums.at[e], dst_ref=zbuf.at[par * GS + w], send_sem=send_sem.at[3], recv_sem=recv_sem.at[3],
            device_id={"date": g * GS + e, "trade": where}, device_id_type=MESH,
        )

    for i in range(1, GS):
        e = lax.rem(w + i, GS)
        sums_copy(e, twin).start()
        sums_copy(e, t).start()
    sums_copy(w, twin).start()
    zbuf[par * GS + w] = sums[w]

    @pl.when(g == 0)
    def _():
        pl.semaphore_wait(ready.at[0], 1)
        total_copy(1, 0, 0).start()
        total_copy(1, 0, 1).wait_recv()
        tmsg[1] = terms(own + twofold(tbuf[1]))
        pl.semaphore_wait(ready.at[1], 1)
        total_copy(3, 1, 0).start()

    @pl.when(g == 1)
    def _():
        tmsg[1] = terms(total)
        pl.semaphore_wait(ready.at[0], 1)
        total_copy(2, 1, 0).start()

    def widen(slot, core):
        for b in range(NB):
            whole = cbuf[slot, core, b].astype(jnp.int32).astype(jnp.float32)
            coarse = jnp.round(whole * np.float32(1 / 256)) * np.float32(256)
            cwide[slot, core, b, :K, :] = coarse.astype(jnp.bfloat16)
            cwide[slot, core, b, K:, :] = (whole - coarse).astype(jnp.bfloat16)

    widen(j, c)
    for i in range(1, NJ):
        slot = lax.rem(j + NJ - i, NJ)
        c_copies[i - 1].wait_recv()
        pass_on(slot).start()
        widen(slot, c)
    bytes_of(cbuf.at[:, c1], recv_sem.at[2], False)
    for slot in range(NJ):
        widen(slot, c1)

    bytes_of(zbuf.at[pl.ds(0, 2 * GS - 1)], recv_sem.at[3], False)
    z = zbuf[...].reshape(2 * GS * SLICE, NB * F)
    pre = jnp.dot(jnp.concatenate([z, z], axis=1), wbuf[...], preferred_element_type=jnp.float32)
    basis = jnp.tanh(pre + offsets).astype(jnp.bfloat16)
    twice = [jnp.concatenate([basis[:, b * K : (b + 1) * K]] * 2, axis=1) for b in range(NB)]

    def final_copy(slot, tc, tp):
        return pltpu.make_async_remote_copy(
            src_ref=part.at[slot, tc], dst_ref=fin.at[j * 4 + c * 2 + p], send_sem=send_sem.at[4], recv_sem=recv_sem.at[4],
            device_id={"trade": slot * 4 + par * 2 + tc, "path": tp}, device_id_type=MESH,
        )

    for i in (2, 1, 3, 0):
        slot = lax.rem(j + i, NJ)
        for b in range(NB):
            both = jnp.concatenate([cwide[slot, 0, b], cwide[slot, 1, b]], axis=1)
            values = jnp.dot(twice[b], both, preferred_element_type=jnp.float32)
            positive = jnp.sum(jnp.maximum(values, 0.0), axis=0, keepdims=True)
            part[slot, 0, b : b + 1, :] = positive[:, :SETS]
            part[slot, 1, b : b + 1, :] = positive[:, SETS:]
        final_copy(slot, c, p1).start()
        final_copy(slot, c1, p1).start()
        final_copy(slot, c1, p).start()
        if i:
            final_copy(slot, c, p).start()

    fin[j * 4 + c * 2 + p] = part[j, c]
    bytes_of(fin.at[pl.ds(0, 15)], recv_sem.at[4], False)
    out[...] = jnp.sum(fin[...], axis=0) * unit[...] * np.float32(1.0 / (GS * SLICE * 32))

    bytes_of(nt.at[pl.ds(0, GS - 1)], send_sem.at[0], True)
    bytes_of(cbuf.at[pl.ds(0, NJ - 1), c], send_sem.at[1], True)
    bytes_of(cbuf.at[:, c], send_sem.at[2], True)
    bytes_of(zbuf.at[pl.ds(0, 2 * GS - 1)], send_sem.at[3], True)
    bytes_of(fin.at[pl.ds(0, 15)], send_sem.at[4], True)

    @pl.when(g < 2)
    def _():
        total_copy(1, 0, 0).wait_send()
        total_copy(1, 1, 0).wait_send()

    @pl.when(g == 2)
    def _():
        bytes_of(nt, send_sem.at[5], True)


def shards(normals, chol, volatility, start_state, basis_map, basis_bias, coef, maturity, netting):
    args = (
        normals, chol, volatility.reshape(1, -1), start_state.reshape(1, -1), basis_map,
        basis_bias.reshape(1, -1), coef, maturity.reshape(1, -1), netting.reshape(1, -1),
    )
    return pl.pallas_call(
        kernel,
        out_shape=jax.ShapeDtypeStruct((NB, SETS), jnp.float32),
        in_specs=[pl.BlockSpec(memory_space=pltpu.HBM)] * len(args),
        out_specs=pl.BlockSpec(memory_space=pltpu.VMEM),
        scratch_shapes=[pltpu.VMEM(a.shape, a.dtype) for a in args]
        + [
            pltpu.VMEM((GS, SLICE, NB * F), jnp.bfloat16),
            pltpu.VMEM((GS, SLICE, NB * F), jnp.bfloat16),
            pltpu.VMEM((GS, SLICE, NB * F), jnp.bfloat16),
            pltpu.VMEM((2, SLICE, NB * F), jnp.bfloat16),
            pltpu.VMEM((2, SLICE, NB * F), jnp.bfloat16),
            pltpu.VMEM((SLICE, NB * F), jnp.float32),
            pltpu.VMEM((GS, SLICE, NB * F), jnp.bfloat16),
            pltpu.VMEM((2 * GS, SLICE, NB * F), jnp.bfloat16),
            pltpu.VMEM((NJ, 2, NB, K, SETS), jnp.int16),
            pltpu.VMEM((NJ, 2, NB, 2 * K, SETS), jnp.bfloat16),
            pltpu.VMEM((NB, SETS), jnp.float32),
            pltpu.VMEM((2 * NB * F, NB * K), jnp.bfloat16),
            pltpu.VMEM((NJ, 2, NB, SETS), jnp.float32),
            pltpu.VMEM((16, NB, SETS), jnp.float32),
            pltpu.SemaphoreType.DMA((len(args),)),
            pltpu.SemaphoreType.DMA((6,)),
            pltpu.SemaphoreType.DMA((6,)),
            pltpu.SemaphoreType.DMA((NJ - 1,)),
            pltpu.SemaphoreType.DMA((2,)),
            pltpu.SemaphoreType.DMA((2,)),
            pltpu.SemaphoreType.REGULAR((2,)),
        ],
        compiler_params=pltpu.CompilerParams(
            collective_id=0, has_side_effects=True, vmem_limit_bytes=60 << 20
        ),
    )(*args)


def solution(mesh):
    placed = (
        P("date", None, ("trade", "path")),
        P(),
        P(),
        P(),
        P(),
        P(),
        P(None, "trade"),
        P("trade"),
        P("trade"),
    )
    return jax.shard_map(
        shards, mesh=mesh, in_specs=placed, out_specs=P("date", "trade"), check_vma=False
    )
```

```python
import jax
import jax.numpy as jnp
import numpy as np
from jax import lax
from jax.experimental import pallas as pl
from jax.experimental.pallas import tpu as pltpu
from jax.sharding import PartitionSpec as P

MESH = pl.DeviceIdType.MESH
ND = 16
NB = 2
F = 64
K = 128
SETS = 128
GS = 4
SLICE = 64
TOP = 127 * 256
NJ = 4
HIGH = lax.Precision.HIGHEST


def kernel(
    normals, chol, vol, start, bmap, bias, coef, mat, net,
    out,
    v_norm, v_chol, v_vol, v_start, v_bmap, v_bias, v_coef, v_mat, v_net,
    nt, arrived, ahead, tmsg, tbuf, base, sums, zbuf, cbuf, cwide, unit, wbuf, part, fin,
    load_sem, send_sem, recv_sem, c_sem, t_sem, t_sent, ready,
):
    d, t, p = lax.axis_index("date"), lax.axis_index("trade"), lax.axis_index("path")
    y, c = lax.div(t, 2), lax.rem(t, 2)
    par = lax.rem(y, 2)
    side = 2 * par - 1
    g, w = lax.div(d, GS), lax.rem(d, GS)
    c1, p1 = 1 - c, 1 - p
    twin = t - 2 * side

    def row(steps):
        return lax.rem(t + 2 * steps + 16, 16)

    def valued(slot):
        return row(side * slot)

    def valuer(slot):
        return row(side * slot * (1 if slot % 2 else -1))

    barrier = pltpu.get_barrier_semaphore()

    def hello(where):
        pl.semaphore_signal(barrier, inc=1, device_id=where, device_id_type=MESH)

    def mate(i):
        return {"date": g * GS + lax.rem(w + i, GS), "path": p1}

    def counterpart(group):
        return {"date": group * GS + w}

    for i in range(GS):
        hello(mate(i))
    for i in (1, 2, 3, -2):
        hello({"trade": row(side * i)})
    hello({"trade": twin})
    other = t + 1 - 2 * c
    hello({"trade": other})
    hello({"trade": other, "path": p1})

    @pl.when(g == 0)
    def _():
        hello(counterpart(1))
        hello(counterpart(3))

    @pl.when(g == 1)
    def _():
        hello(counterpart(2))

    @pl.when(g == 3)
    def _():
        for i in range(GS):
            hello({"date": 2 * GS + i, "path": p1})

    loads = [
        pltpu.make_async_copy(a, b, load_sem.at[i])
        for i, (a, b) in enumerate(
            (
                (normals, v_norm), (coef, v_coef), (mat, v_mat), (net, v_net), (chol, v_chol),
                (vol, v_vol), (start, v_start), (bmap, v_bmap), (bias, v_bias),
            )
        )
    ]
    for load in loads:
        load.start()

    loads[0].wait()
    flat = v_norm[...].reshape(NB * F, GS * SLICE).astype(jnp.float32)
    nt[...] = flat.T.astype(jnp.bfloat16).reshape(GS, SLICE, NB * F)

    for load in loads[1:4]:
        load.wait()
    local_set = v_net[...] - t * SETS
    trades = v_coef.shape[1]
    member = (lax.broadcasted_iota(jnp.int32, (SETS, trades), 0) == local_set)
    member = member.astype(jnp.float32).astype(jnp.bfloat16)
    for b in range(NB):
        alive = (d * NB + b < v_mat[...]).astype(jnp.float32).astype(jnp.bfloat16)
        folded = lax.dot_general(
            v_coef[...] * alive, member, (((1,), (1,)), ((), ())), preferred_element_type=jnp.float32
        )
        largest = jnp.maximum(jnp.max(jnp.abs(folded), axis=0, keepdims=True), np.float32(1e-30))
        unit[b : b + 1, :] = largest * np.float32(1.0 / TOP)
        cbuf[0, c, b] = jnp.round(folded * (np.float32(TOP) / largest)).astype(jnp.int32).astype(jnp.int16)

    heard = jnp.where(g == 0, 0, 1) + jnp.where(g == 2, GS, 0)
    pl.semaphore_wait(barrier, GS + 4 + 3 + heard)

    for i in (2, 3, 1, 0):
        pltpu.make_async_remote_copy(
            src_ref=nt.at[lax.rem(w + i, GS)], dst_ref=arrived.at[w], send_sem=send_sem.at[0], recv_sem=recv_sem.at[0],
            device_id=mate(i), device_id_type=MESH,
        ).start()

    @pl.when(g == 2)
    def _():
        for i in range(GS):
            pltpu.make_async_remote_copy(
                src_ref=nt.at[i], dst_ref=ahead.at[w], send_sem=send_sem.at[5], recv_sem=recv_sem.at[5],
                device_id={"date": 3 * GS + i, "path": p1}, device_id_type=MESH,
            ).start()

    def say_ready(to, slot):
        pl.semaphore_signal(ready.at[slot], inc=1, device_id=counterpart(to), device_id_type=MESH)

    @pl.when(g == 1)
    def _():
        say_ready(0, 0)

    @pl.when(g == 2)
    def _():
        say_ready(1, 0)

    @pl.when(g == 3)
    def _():
        say_ready(0, 1)

    c_copies = [
        pltpu.make_async_remote_copy(
            src_ref=cbuf.at[0, c], dst_ref=cbuf.at[i, c], send_sem=send_sem.at[1], recv_sem=c_sem.at[i - 1],
            device_id={"trade": valuer(i)}, device_id_type=MESH,
        )
        for i in range(1, NJ)
    ]
    for copy in c_copies:
        copy.start()

    def pass_on(slot):
        return pltpu.make_async_remote_copy(
            src_ref=cbuf.at[slot, c], dst_ref=cbuf.at[slot, c], send_sem=send_sem.at[2], recv_sem=recv_sem.at[2],
            device_id={"trade": other}, device_id_type=MESH,
        )

    pass_on(0).start()

    for load in loads[4:]:
        load.wait()
    scale = v_vol[...] * np.float32(np.sqrt(np.float32(1.0) / np.float32(ND * NB)))
    joint = jnp.dot(v_chol[...].T * scale, v_bmap[...], precision=HIGH, preferred_element_type=jnp.float32)
    offset = jnp.dot(v_start[...], v_bmap[...], precision=HIGH, preferred_element_type=jnp.float32) + v_bias[...]
    joint_high = joint.astype(jnp.bfloat16)
    joint_low = (joint - joint_high.astype(jnp.float32)).astype(jnp.bfloat16)
    wbuf[...] = jnp.zeros_like(wbuf)
    for b in range(NB):
        wbuf[pl.ds(b * F, F), pl.ds(b * K, K)] = joint_high
        wbuf[pl.ds(NB * F + b * F, F), pl.ds(b * K, K)] = joint_low
    offsets = jnp.concatenate([offset, offset], axis=1)

    def bytes_of(ref, sem, send):
        whole = pltpu.make_async_remote_copy(
            src_ref=ref, dst_ref=ref, send_sem=sem, recv_sem=sem, device_id={"trade": other}, device_id_type=MESH
        )
        return whole.wait_send() if send else whole.wait_recv()

    bytes_of(arrived, recv_sem.at[0], False)
    later_half = lax.broadcasted_iota(jnp.int32, (SLICE, NB * F), 1) >= F

    def twofold(message):
        message = message.astype(jnp.float32)
        return message + pltpu.roll(message, F, axis=1)

    def terms(value):
        high = value.astype(jnp.bfloat16).astype(jnp.float32)
        return jnp.where(later_half, value - high, value).astype(jnp.bfloat16)

    own = sum(twofold(arrived[e]) for e in range(GS))
    tmsg[0] = terms(own)

    def total_copy(to, message, slot):
        return pltpu.make_async_remote_copy(
            src_ref=tmsg.at[message], dst_ref=tbuf.at[slot], send_sem=t_sent.at[message], recv_sem=t_sem.at[slot],
            device_id=counterpart(to), device_id_type=MESH,
        )

    @pl.when(g == 0)
    def _():
        base[...] = jnp.zeros_like(base)

    @pl.when(g == 1)
    def _():
        total_copy(0, 0, 1).start()

    @pl.when(g > 0)
    def _():
        total_copy(0, 0, 0).wait_recv()
        base[...] = twofold(tbuf[0])

    @pl.when(g == 3)
    def _():
        bytes_of(ahead, recv_sem.at[5], False)
        base[...] += sum(twofold(ahead[e]) for e in range(GS))

    total = base[...]
    for e in range(GS):
        block = arrived[e].astype(jnp.float32)
        pair = block + pltpu.roll(block, F, axis=1)
        sums[e] = (total + jnp.where(later_half, pair, block)).astype(jnp.bfloat16)
        total = total + pair

    for i in (2, 3, 1, 0):
        for where in (twin, t):
            pltpu.make_async_remote_copy(
                src_ref=sums.at[lax.rem(w + i, GS)], dst_ref=zbuf.at[par * GS + w], send_sem=send_sem.at[3], recv_sem=recv_sem.at[3],
                device_id={**mate(i), "trade": where}, device_id_type=MESH,
            ).start()

    @pl.when(g == 0)
    def _():
        pl.semaphore_wait(ready.at[0], 1)
        total_copy(1, 0, 0).start()
        total_copy(1, 0, 1).wait_recv()
        tmsg[1] = terms(own + twofold(tbuf[1]))
        pl.semaphore_wait(ready.at[1], 1)
        total_copy(3, 1, 0).start()

    @pl.when(g == 1)
    def _():
        tmsg[1] = terms(total)
        pl.semaphore_wait(ready.at[0], 1)
        total_copy(2, 1, 0).start()

    def widen(slot, core):
        for b in range(NB):
            whole = cbuf[slot, core, b].astype(jnp.int32).astype(jnp.float32)
            coarse = jnp.round(whole * np.float32(1 / 256)) * np.float32(256)
            cwide[slot, core, b, :K, :] = coarse.astype(jnp.bfloat16)
            cwide[slot, core, b, K:, :] = (whole - coarse).astype(jnp.bfloat16)

    widen(0, c)
    for slot in range(1, NJ):
        c_copies[slot - 1].wait_recv()
        pass_on(slot).start()
        widen(slot, c)
    bytes_of(cbuf.at[:, c1], recv_sem.at[2], False)
    for slot in range(NJ):
        widen(slot, c1)

    bytes_of(zbuf, recv_sem.at[3], False)
    z = zbuf[...].reshape(2 * GS * SLICE, NB * F)
    pre = jnp.dot(jnp.concatenate([z, z], axis=1), wbuf[...], preferred_element_type=jnp.float32)
    basis = jnp.tanh(pre + offsets).astype(jnp.bfloat16)
    twice = [jnp.concatenate([basis[:, b * K : (b + 1) * K]] * 2, axis=1) for b in range(NB)]

    for slot in range(NJ - 1, -1, -1):
        for b in range(NB):
            both = jnp.concatenate([cwide[slot, 0, b], cwide[slot, 1, b]], axis=1)
            values = jnp.dot(twice[b], both, preferred_element_type=jnp.float32)
            positive = jnp.sum(jnp.maximum(values, 0.0), axis=0, keepdims=True)
            part[slot, 0, b : b + 1, :] = positive[:, :SETS]
            part[slot, 1, b : b + 1, :] = positive[:, SETS:]
        for tc, tp in ((c1, p1), (c, p1), (c1, p), (c, p))[: 4 if slot else 3]:
            pltpu.make_async_remote_copy(
                src_ref=part.at[slot, tc], dst_ref=fin.at[slot * 4 + c * 2 + p], send_sem=send_sem.at[4], recv_sem=recv_sem.at[4],
                device_id={"trade": valued(slot) - c + tc, "path": tp}, device_id_type=MESH,
            ).start()

    fin[c * 2 + p] = part[0, c]
    bytes_of(fin.at[pl.ds(0, 15)], recv_sem.at[4], False)
    out[...] = jnp.sum(fin[...], axis=0) * unit[...] * np.float32(1.0 / (GS * SLICE * 32))

    bytes_of(nt, send_sem.at[0], True)
    bytes_of(cbuf.at[pl.ds(0, NJ - 1), c], send_sem.at[1], True)
    bytes_of(cbuf.at[:, c], send_sem.at[2], True)
    bytes_of(zbuf, send_sem.at[3], True)
    bytes_of(fin.at[pl.ds(0, 15)], send_sem.at[4], True)

    @pl.when(g < 2)
    def _():
        total_copy(1, 0, 0).wait_send()
        total_copy(1, 1, 0).wait_send()

    @pl.when(g == 2)
    def _():
        bytes_of(nt, send_sem.at[5], True)


def shards(normals, chol, volatility, start_state, basis_map, basis_bias, coef, maturity, netting):
    args = (
        normals, chol, volatility.reshape(1, -1), start_state.reshape(1, -1), basis_map,
        basis_bias.reshape(1, -1), coef, maturity.reshape(1, -1), netting.reshape(1, -1),
    )
    return pl.pallas_call(
        kernel,
        out_shape=jax.ShapeDtypeStruct((NB, SETS), jnp.float32),
        in_specs=[pl.BlockSpec(memory_space=pltpu.HBM)] * len(args),
        out_specs=pl.BlockSpec(memory_space=pltpu.VMEM),
        scratch_shapes=[pltpu.VMEM(a.shape, a.dtype) for a in args]
        + [
            pltpu.VMEM((GS, SLICE, NB * F), jnp.bfloat16),
            pltpu.VMEM((GS, SLICE, NB * F), jnp.bfloat16),
            pltpu.VMEM((GS, SLICE, NB * F), jnp.bfloat16),
            pltpu.VMEM((2, SLICE, NB * F), jnp.bfloat16),
            pltpu.VMEM((2, SLICE, NB * F), jnp.bfloat16),
            pltpu.VMEM((SLICE, NB * F), jnp.float32),
            pltpu.VMEM((GS, SLICE, NB * F), jnp.bfloat16),
            pltpu.VMEM((2 * GS, SLICE, NB * F), jnp.bfloat16),
            pltpu.VMEM((NJ, 2, NB, K, SETS), jnp.int16),
            pltpu.VMEM((NJ, 2, NB, 2 * K, SETS), jnp.bfloat16),
            pltpu.VMEM((NB, SETS), jnp.float32),
            pltpu.VMEM((2 * NB * F, NB * K), jnp.bfloat16),
            pltpu.VMEM((NJ, 2, NB, SETS), jnp.float32),
            pltpu.VMEM((16, NB, SETS), jnp.float32),
            pltpu.SemaphoreType.DMA((len(args),)),
            pltpu.SemaphoreType.DMA((6,)),
            pltpu.SemaphoreType.DMA((6,)),
            pltpu.SemaphoreType.DMA((NJ - 1,)),
            pltpu.SemaphoreType.DMA((2,)),
            pltpu.SemaphoreType.DMA((2,)),
            pltpu.SemaphoreType.REGULAR((2,)),
        ],
        compiler_params=pltpu.CompilerParams(
            collective_id=0, has_side_effects=True, vmem_limit_bytes=60 << 20
        ),
    )(*args)


def solution(mesh):
    placed = (
        P("date", None, ("trade", "path")),
        P(),
        P(),
        P(),
        P(),
        P(),
        P(None, "trade"),
        P("trade"),
        P("trade"),
    )
    return jax.shard_map(
        shards, mesh=mesh, in_specs=placed, out_specs=P("date", "trade"), check_vma=False
    )
```

```python
import jax
import jax.numpy as jnp
import numpy as np
from jax import lax
from jax.experimental import pallas as pl
from jax.experimental.pallas import tpu as pltpu
from jax.sharding import PartitionSpec as P

MESH = pl.DeviceIdType.MESH
ND = 16
NB = 2
F = 64
K = 128
SETS = 128
GS = 4
SLICE = 64
TOP = 127 * 256
NJ = 4
HIGH = lax.Precision.HIGHEST


def kernel(
    normals, chol, vol, start, bmap, bias, coef, mat, net,
    out,
    v_norm, v_chol, v_vol, v_start, v_bmap, v_bias, v_coef, v_mat, v_net,
    nt, arrived, ahead, tmsg, tbuf, base, sums, zbuf, cbuf, cwide, unit, wbuf, part, fin,
    load_sem, send_sem, recv_sem, c_sem, t_sem, t_sent, ready,
):
    d, t, p = lax.axis_index("date"), lax.axis_index("trade"), lax.axis_index("path")
    y, c = lax.div(t, 2), lax.rem(t, 2)
    par = lax.rem(y, 2)
    side = 2 * par - 1
    g, w = lax.div(d, GS), lax.rem(d, GS)
    c1, p1 = 1 - c, 1 - p
    twin = t - 2 * side

    def row(steps):
        return lax.rem(t + 2 * steps + 16, 16)

    def valued(slot):
        return row(side * slot)

    def valuer(slot):
        return row(side * slot * (1 if slot % 2 else -1))

    barrier = pltpu.get_barrier_semaphore()

    def hello(where):
        pl.semaphore_signal(barrier, inc=1, device_id=where, device_id_type=MESH)

    def mate(i):
        return {"date": g * GS + lax.rem(w + i, GS), "path": p1}

    def counterpart(group):
        return {"date": group * GS + w}

    for i in range(GS):
        hello(mate(i))
    for i in (1, 2, 3, -2):
        hello({"trade": row(side * i)})
    hello({"trade": twin})
    other = t + 1 - 2 * c
    hello({"trade": other})
    hello({"trade": other, "path": p1})

    @pl.when(g == 0)
    def _():
        hello(counterpart(1))
        hello(counterpart(3))

    @pl.when(g == 1)
    def _():
        hello(counterpart(2))

    outer = jnp.logical_or(g == 0, g == 3)
    beside = jnp.where(g < 2, 1 - g, 5 - g)

    def across(i):
        return {"date": beside * GS + lax.rem(w + i, GS), "path": p1}

    @pl.when(outer)
    def _():
        for i in range(GS):
            hello(across(i))

    loads = [
        pltpu.make_async_copy(a, b, load_sem.at[i])
        for i, (a, b) in enumerate(
            (
                (normals, v_norm), (coef, v_coef), (mat, v_mat), (net, v_net), (chol, v_chol),
                (vol, v_vol), (start, v_start), (bmap, v_bmap), (bias, v_bias),
            )
        )
    ]
    for load in loads:
        load.start()

    loads[0].wait()
    flat = v_norm[...].reshape(NB * F, GS * SLICE).astype(jnp.float32)
    nt[...] = flat.T.astype(jnp.bfloat16).reshape(GS, SLICE, NB * F)

    for load in loads[1:4]:
        load.wait()
    local_set = v_net[...] - t * SETS
    trades = v_coef.shape[1]
    member = (lax.broadcasted_iota(jnp.int32, (SETS, trades), 0) == local_set)
    member = member.astype(jnp.float32).astype(jnp.bfloat16)
    for b in range(NB):
        alive = (d * NB + b < v_mat[...]).astype(jnp.float32).astype(jnp.bfloat16)
        folded = lax.dot_general(
            v_coef[...] * alive, member, (((1,), (1,)), ((), ())), preferred_element_type=jnp.float32
        )
        largest = jnp.maximum(jnp.max(jnp.abs(folded), axis=0, keepdims=True), np.float32(1e-30))
        unit[b : b + 1, :] = largest * np.float32(1.0 / TOP)
        cbuf[0, c, b] = jnp.round(folded * (np.float32(TOP) / largest)).astype(jnp.int32).astype(jnp.int16)

    heard = jnp.where(g == 0, 0, 1) + jnp.where(outer, 0, GS)
    pl.semaphore_wait(barrier, GS + 4 + 3 + heard)

    for i in (2, 3, 1, 0):
        pltpu.make_async_remote_copy(
            src_ref=nt.at[lax.rem(w + i, GS)], dst_ref=arrived.at[w], send_sem=send_sem.at[0], recv_sem=recv_sem.at[0],
            device_id=mate(i), device_id_type=MESH,
        ).start()

    @pl.when(jnp.logical_not(outer))
    def _():
        for i in range(GS):
            pltpu.make_async_remote_copy(
                src_ref=nt.at[lax.rem(w + i, GS)], dst_ref=ahead.at[w], send_sem=send_sem.at[5], recv_sem=recv_sem.at[5],
                device_id=across(i), device_id_type=MESH,
            ).start()

    def say_ready(to, slot):
        pl.semaphore_signal(ready.at[slot], inc=1, device_id=counterpart(to), device_id_type=MESH)

    @pl.when(g == 1)
    def _():
        say_ready(0, 0)

    @pl.when(g == 2)
    def _():
        say_ready(1, 0)

    @pl.when(g == 3)
    def _():
        say_ready(0, 1)

    c_copies = [
        pltpu.make_async_remote_copy(
            src_ref=cbuf.at[0, c], dst_ref=cbuf.at[i, c], send_sem=send_sem.at[1], recv_sem=c_sem.at[i - 1],
            device_id={"trade": valuer(i)}, device_id_type=MESH,
        )
        for i in range(1, NJ)
    ]
    for copy in c_copies:
        copy.start()

    def pass_on(slot):
        return pltpu.make_async_remote_copy(
            src_ref=cbuf.at[slot, c], dst_ref=cbuf.at[slot, c], send_sem=send_sem.at[2], recv_sem=recv_sem.at[2],
            device_id={"trade": other}, device_id_type=MESH,
        )

    pass_on(0).start()

    for load in loads[4:]:
        load.wait()
    scale = v_vol[...] * np.float32(np.sqrt(np.float32(1.0) / np.float32(ND * NB)))
    joint = jnp.dot(v_chol[...].T * scale, v_bmap[...], precision=HIGH, preferred_element_type=jnp.float32)
    offset = jnp.dot(v_start[...], v_bmap[...], precision=HIGH, preferred_element_type=jnp.float32) + v_bias[...]
    joint_high = joint.astype(jnp.bfloat16)
    joint_low = (joint - joint_high.astype(jnp.float32)).astype(jnp.bfloat16)
    wbuf[...] = jnp.zeros_like(wbuf)
    for b in range(NB):
        wbuf[pl.ds(b * F, F), pl.ds(b * K, K)] = joint_high
        wbuf[pl.ds(NB * F + b * F, F), pl.ds(b * K, K)] = joint_low
    offsets = jnp.concatenate([offset, offset], axis=1)

    def bytes_of(ref, sem, send):
        whole = pltpu.make_async_remote_copy(
            src_ref=ref, dst_ref=ref, send_sem=sem, recv_sem=sem, device_id={"trade": other}, device_id_type=MESH
        )
        return whole.wait_send() if send else whole.wait_recv()

    bytes_of(arrived, recv_sem.at[0], False)
    later_half = lax.broadcasted_iota(jnp.int32, (SLICE, NB * F), 1) >= F

    def twofold(message):
        message = message.astype(jnp.float32)
        return message + pltpu.roll(message, F, axis=1)

    def terms(value):
        high = value.astype(jnp.bfloat16).astype(jnp.float32)
        return jnp.where(later_half, value - high, value).astype(jnp.bfloat16)

    own = sum(twofold(arrived[e]) for e in range(GS))
    tmsg[0] = terms(own)

    def total_copy(to, message):
        return pltpu.make_async_remote_copy(
            src_ref=tmsg.at[message], dst_ref=tbuf, send_sem=t_sent.at[message], recv_sem=t_sem.at[0],
            device_id=counterpart(to), device_id_type=MESH,
        )

    @pl.when(g == 0)
    def _():
        base[...] = jnp.zeros_like(base)

    @pl.when(g > 0)
    def _():
        total_copy(0, 0).wait_recv()
        base[...] = twofold(tbuf[...])

    @pl.when(g == 3)
    def _():
        bytes_of(ahead, recv_sem.at[5], False)
        base[...] += sum(twofold(ahead[e]) for e in range(GS))

    total = base[...]
    for e in range(GS):
        block = arrived[e].astype(jnp.float32)
        pair = block + pltpu.roll(block, F, axis=1)
        sums[e] = (total + jnp.where(later_half, pair, block)).astype(jnp.bfloat16)
        total = total + pair

    for i in (2, 3, 1, 0):
        for where in (twin, t):
            pltpu.make_async_remote_copy(
                src_ref=sums.at[lax.rem(w + i, GS)], dst_ref=zbuf.at[par * GS + w], send_sem=send_sem.at[3], recv_sem=recv_sem.at[3],
                device_id={**mate(i), "trade": where}, device_id_type=MESH,
            ).start()

    @pl.when(g == 0)
    def _():
        pl.semaphore_wait(ready.at[0], 1)
        total_copy(1, 0).start()
        bytes_of(ahead, recv_sem.at[5], False)
        tmsg[1] = terms(own + sum(twofold(ahead[e]) for e in range(GS)))
        pl.semaphore_wait(ready.at[1], 1)
        total_copy(3, 1).start()

    @pl.when(g == 1)
    def _():
        tmsg[1] = terms(total)
        pl.semaphore_wait(ready.at[0], 1)
        total_copy(2, 1).start()

    def widen(slot, core):
        for b in range(NB):
            whole = cbuf[slot, core, b].astype(jnp.int32).astype(jnp.float32)
            coarse = jnp.round(whole * np.float32(1 / 256)) * np.float32(256)
            cwide[slot, core, b, :K, :] = coarse.astype(jnp.bfloat16)
            cwide[slot, core, b, K:, :] = (whole - coarse).astype(jnp.bfloat16)

    widen(0, c)
    for slot in range(1, NJ):
        c_copies[slot - 1].wait_recv()
        pass_on(slot).start()
        widen(slot, c)
    bytes_of(cbuf.at[:, c1], recv_sem.at[2], False)
    for slot in range(NJ):
        widen(slot, c1)

    bytes_of(zbuf, recv_sem.at[3], False)
    z = zbuf[...].reshape(2 * GS * SLICE, NB * F)
    pre = jnp.dot(jnp.concatenate([z, z], axis=1), wbuf[...], preferred_element_type=jnp.float32)
    basis = jnp.tanh(pre + offsets).astype(jnp.bfloat16)
    twice = [jnp.concatenate([basis[:, b * K : (b + 1) * K]] * 2, axis=1) for b in range(NB)]

    for slot in range(NJ - 1, -1, -1):
        for b in range(NB):
            both = jnp.concatenate([cwide[slot, 0, b], cwide[slot, 1, b]], axis=1)
            values = jnp.dot(twice[b], both, preferred_element_type=jnp.float32)
            positive = jnp.sum(jnp.maximum(values, 0.0), axis=0, keepdims=True)
            part[slot, 0, b : b + 1, :] = positive[:, :SETS]
            part[slot, 1, b : b + 1, :] = positive[:, SETS:]
        for tc, tp in ((c1, p1), (c, p1), (c1, p), (c, p))[: 4 if slot else 3]:
            pltpu.make_async_remote_copy(
                src_ref=part.at[slot, tc], dst_ref=fin.at[slot * 4 + c * 2 + p], send_sem=send_sem.at[4], recv_sem=recv_sem.at[4],
                device_id={"trade": valued(slot) - c + tc, "path": tp}, device_id_type=MESH,
            ).start()

    fin[c * 2 + p] = part[0, c]
    bytes_of(fin.at[pl.ds(0, 15)], recv_sem.at[4], False)
    out[...] = jnp.sum(fin[...], axis=0) * unit[...] * np.float32(1.0 / (GS * SLICE * 32))

    bytes_of(nt, send_sem.at[0], True)
    bytes_of(cbuf.at[pl.ds(0, NJ - 1), c], send_sem.at[1], True)
    bytes_of(cbuf.at[:, c], send_sem.at[2], True)
    bytes_of(zbuf, send_sem.at[3], True)
    bytes_of(fin.at[pl.ds(0, 15)], send_sem.at[4], True)

    @pl.when(g == 0)
    def _():
        total_copy(1, 0).wait_send()

    @pl.when(g < 2)
    def _():
        total_copy(1, 1).wait_send()

    @pl.when(jnp.logical_not(outer))
    def _():
        bytes_of(nt, send_sem.at[5], True)


def shards(normals, chol, volatility, start_state, basis_map, basis_bias, coef, maturity, netting):
    args = (
        normals, chol, volatility.reshape(1, -1), start_state.reshape(1, -1), basis_map,
        basis_bias.reshape(1, -1), coef, maturity.reshape(1, -1), netting.reshape(1, -1),
    )
    return pl.pallas_call(
        kernel,
        out_shape=jax.ShapeDtypeStruct((NB, SETS), jnp.float32),
        in_specs=[pl.BlockSpec(memory_space=pltpu.HBM)] * len(args),
        out_specs=pl.BlockSpec(memory_space=pltpu.VMEM),
        scratch_shapes=[pltpu.VMEM(a.shape, a.dtype) for a in args]
        + [
            pltpu.VMEM((GS, SLICE, NB * F), jnp.bfloat16),
            pltpu.VMEM((GS, SLICE, NB * F), jnp.bfloat16),
            pltpu.VMEM((GS, SLICE, NB * F), jnp.bfloat16),
            pltpu.VMEM((2, SLICE, NB * F), jnp.bfloat16),
            pltpu.VMEM((SLICE, NB * F), jnp.bfloat16),
            pltpu.VMEM((SLICE, NB * F), jnp.float32),
            pltpu.VMEM((GS, SLICE, NB * F), jnp.bfloat16),
            pltpu.VMEM((2 * GS, SLICE, NB * F), jnp.bfloat16),
            pltpu.VMEM((NJ, 2, NB, K, SETS), jnp.int16),
            pltpu.VMEM((NJ, 2, NB, 2 * K, SETS), jnp.bfloat16),
            pltpu.VMEM((NB, SETS), jnp.float32),
            pltpu.VMEM((2 * NB * F, NB * K), jnp.bfloat16),
            pltpu.VMEM((NJ, 2, NB, SETS), jnp.float32),
            pltpu.VMEM((16, NB, SETS), jnp.float32),
            pltpu.SemaphoreType.DMA((len(args),)),
            pltpu.SemaphoreType.DMA((6,)),
            pltpu.SemaphoreType.DMA((6,)),
            pltpu.SemaphoreType.DMA((NJ - 1,)),
            pltpu.SemaphoreType.DMA((1,)),
            pltpu.SemaphoreType.DMA((2,)),
            pltpu.SemaphoreType.REGULAR((2,)),
        ],
        compiler_params=pltpu.CompilerParams(
            collective_id=0, has_side_effects=True, vmem_limit_bytes=60 << 20
        ),
    )(*args)


def solution(mesh):
    placed = (
        P("date", None, ("trade", "path")),
        P(),
        P(),
        P(),
        P(),
        P(),
        P(None, "trade"),
        P("trade"),
        P("trade"),
    )
    return jax.shard_map(
        shards, mesh=mesh, in_specs=placed, out_specs=P("date", "trade"), check_vma=False
    )
```

```python
import jax
import jax.numpy as jnp
import numpy as np
from jax import lax
from jax.experimental import pallas as pl
from jax.experimental.pallas import tpu as pltpu
from jax.sharding import PartitionSpec as P

MESH = pl.DeviceIdType.MESH
ND = 16
NB = 2
F = 64
K = 128
SETS = 128
GS = 4
SLICE = 64
TOP = 127 * 256
NJ = 4
HIGH = lax.Precision.HIGHEST


def kernel(
    normals, chol, vol, start, bmap, bias, coef, mat, net,
    out,
    v_norm, v_chol, v_vol, v_start, v_bmap, v_bias, v_coef, v_mat, v_net,
    nt, arrived, ahead, tmsg, tbuf, base, sums, zbuf, cbuf, cwide, unit, wbuf, part, fin,
    load_sem, send_sem, recv_sem, c_sem, t_sem, t_sent, ready,
):
    d, t, p = lax.axis_index("date"), lax.axis_index("trade"), lax.axis_index("path")
    y, c = lax.div(t, 2), lax.rem(t, 2)
    par = lax.rem(y, 2)
    side = 2 * par - 1
    g, w = lax.div(d, GS), lax.rem(d, GS)
    c1, p1 = 1 - c, 1 - p
    twin = t - 2 * side

    def row(steps):
        return lax.rem(t + 2 * steps + 16, 16)

    def valued(slot):
        return row(side * slot)

    def valuer(slot):
        return row(side * slot * (1 if slot % 2 else -1))

    barrier = pltpu.get_barrier_semaphore()

    def hello(where):
        pl.semaphore_signal(barrier, inc=1, device_id=where, device_id_type=MESH)

    def mate(i):
        return {"date": g * GS + lax.rem(w + i, GS), "path": p1}

    def counterpart(group):
        return {"date": group * GS + w}

    for i in range(GS):
        hello(mate(i))
    for i in (1, 2, 3, -2):
        hello({"trade": row(side * i)})
    hello({"trade": twin})
    other = t + 1 - 2 * c
    hello({"trade": other})
    hello({"trade": other, "path": p1})

    @pl.when(g == 0)
    def _():
        hello(counterpart(1))
        hello(counterpart(3))

    @pl.when(g == 1)
    def _():
        hello(counterpart(2))

    outer = jnp.logical_or(g == 0, g == 3)
    beside = jnp.where(g < 2, 1 - g, 5 - g)

    def across(i):
        return {"date": beside * GS + lax.rem(w + i, GS), "path": p1}

    @pl.when(outer)
    def _():
        for i in range(GS):
            hello(across(i))

    loads = [
        pltpu.make_async_copy(a, b, load_sem.at[i])
        for i, (a, b) in enumerate(
            (
                (normals, v_norm), (coef, v_coef), (mat, v_mat), (net, v_net), (chol, v_chol),
                (vol, v_vol), (start, v_start), (bmap, v_bmap), (bias, v_bias),
            )
        )
    ]
    for load in loads:
        load.start()

    loads[0].wait()
    flat = v_norm[...].reshape(NB * F, GS * SLICE).astype(jnp.float32)
    nt[...] = flat.T.astype(jnp.bfloat16).reshape(GS, SLICE, NB * F)

    for load in loads[1:4]:
        load.wait()
    local_set = v_net[...] - t * SETS
    trades = v_coef.shape[1]
    member = (lax.broadcasted_iota(jnp.int32, (SETS, trades), 0) == local_set)
    member = member.astype(jnp.float32).astype(jnp.bfloat16)
    for b in range(NB):
        alive = (d * NB + b < v_mat[...]).astype(jnp.float32).astype(jnp.bfloat16)
        folded = lax.dot_general(
            v_coef[...] * alive, member, (((1,), (1,)), ((), ())), preferred_element_type=jnp.float32
        )
        largest = jnp.maximum(jnp.max(jnp.abs(folded), axis=0, keepdims=True), np.float32(1e-30))
        unit[b : b + 1, :] = largest * np.float32(1.0 / TOP)
        cbuf[0, c, b] = jnp.round(folded * (np.float32(TOP) / largest)).astype(jnp.int32).astype(jnp.int16)

    heard = jnp.where(g == 0, 0, 1) + jnp.where(outer, 0, GS)
    pl.semaphore_wait(barrier, GS + 4 + 3 + heard)

    for i in (2, 3, 1, 0):
        pltpu.make_async_remote_copy(
            src_ref=nt.at[lax.rem(w + i, GS)], dst_ref=arrived.at[w], send_sem=send_sem.at[0], recv_sem=recv_sem.at[0],
            device_id=mate(i), device_id_type=MESH,
        ).start()

    @pl.when(jnp.logical_not(outer))
    def _():
        for i in range(GS):
            pltpu.make_async_remote_copy(
                src_ref=nt.at[lax.rem(w + i, GS)], dst_ref=ahead.at[w], send_sem=send_sem.at[5], recv_sem=recv_sem.at[5],
                device_id=across(i), device_id_type=MESH,
            ).start()

    def say_ready(to, slot):
        pl.semaphore_signal(ready.at[slot], inc=1, device_id=counterpart(to), device_id_type=MESH)

    @pl.when(g == 1)
    def _():
        say_ready(0, 0)

    @pl.when(g == 2)
    def _():
        say_ready(1, 0)

    @pl.when(g == 3)
    def _():
        say_ready(0, 1)

    c_copies = [
        pltpu.make_async_remote_copy(
            src_ref=cbuf.at[0, c], dst_ref=cbuf.at[i, c], send_sem=send_sem.at[1], recv_sem=c_sem.at[i - 1],
            device_id={"trade": valuer(i)}, device_id_type=MESH,
        )
        for i in range(1, NJ)
    ]
    for copy in c_copies:
        copy.start()

    def pass_on(slot):
        return pltpu.make_async_remote_copy(
            src_ref=cbuf.at[slot, c], dst_ref=cbuf.at[slot, c], send_sem=send_sem.at[2], recv_sem=recv_sem.at[2],
            device_id={"trade": other}, device_id_type=MESH,
        )

    pass_on(0).start()

    for load in loads[4:]:
        load.wait()
    scale = v_vol[...] * np.float32(np.sqrt(np.float32(1.0) / np.float32(ND * NB)))
    joint = jnp.dot(v_chol[...].T * scale, v_bmap[...], precision=HIGH, preferred_element_type=jnp.float32)
    offset = jnp.dot(v_start[...], v_bmap[...], precision=HIGH, preferred_element_type=jnp.float32) + v_bias[...]
    joint_high = joint.astype(jnp.bfloat16)
    joint_low = (joint - joint_high.astype(jnp.float32)).astype(jnp.bfloat16)
    wbuf[...] = jnp.zeros_like(wbuf)
    for b in range(NB):
        wbuf[pl.ds(b * F, F), pl.ds(b * K, K)] = joint_high
        wbuf[pl.ds(NB * F + b * F, F), pl.ds(b * K, K)] = joint_low
    offsets = jnp.concatenate([offset, offset], axis=1)

    def bytes_of(ref, sem, send):
        whole = pltpu.make_async_remote_copy(
            src_ref=ref, dst_ref=ref, send_sem=sem, recv_sem=sem, device_id={"trade": other}, device_id_type=MESH
        )
        return whole.wait_send() if send else whole.wait_recv()

    bytes_of(arrived, recv_sem.at[0], False)
    later_half = lax.broadcasted_iota(jnp.int32, (SLICE, NB * F), 1) >= F

    def twofold(message):
        message = message.astype(jnp.float32)
        return message + pltpu.roll(message, F, axis=1)

    def terms(value):
        high = value.astype(jnp.bfloat16).astype(jnp.float32)
        return jnp.where(later_half, value - high, value).astype(jnp.bfloat16)

    own = sum(twofold(arrived[e]) for e in range(GS))
    tmsg[0] = terms(own)

    def total_copy(to, message):
        return pltpu.make_async_remote_copy(
            src_ref=tmsg.at[message], dst_ref=tbuf, send_sem=t_sent.at[message], recv_sem=t_sem.at[0],
            device_id=counterpart(to), device_id_type=MESH,
        )

    @pl.when(g == 0)
    def _():
        base[...] = jnp.zeros_like(base)

    @pl.when(g > 0)
    def _():
        total_copy(0, 0).wait_recv()
        base[...] = twofold(tbuf[...])

    @pl.when(g == 3)
    def _():
        bytes_of(ahead, recv_sem.at[5], False)
        base[...] += sum(twofold(ahead[e]) for e in range(GS))

    total = base[...]
    for e in range(GS):
        block = arrived[e].astype(jnp.float32)
        pair = block + pltpu.roll(block, F, axis=1)
        sums[e] = (total + jnp.where(later_half, pair, block)).astype(jnp.bfloat16)
        total = total + pair

    for i in (2, 3, 1, 0):
        for where in (twin, t):
            pltpu.make_async_remote_copy(
                src_ref=sums.at[lax.rem(w + i, GS)], dst_ref=zbuf.at[par * GS + w], send_sem=send_sem.at[3], recv_sem=recv_sem.at[3],
                device_id={**mate(i), "trade": where}, device_id_type=MESH,
            ).start()

    @pl.when(g == 0)
    def _():
        pl.semaphore_wait(ready.at[0], 1)
        total_copy(1, 0).start()
        bytes_of(ahead, recv_sem.at[5], False)
        tmsg[1] = terms(own + sum(twofold(ahead[e]) for e in range(GS)))
        pl.semaphore_wait(ready.at[1], 1)
        total_copy(3, 1).start()

    @pl.when(g == 1)
    def _():
        tmsg[1] = terms(total)
        pl.semaphore_wait(ready.at[0], 1)
        total_copy(2, 1).start()

    def widen(slot, core):
        for b in range(NB):
            whole = cbuf[slot, core, b].astype(jnp.int32).astype(jnp.float32)
            coarse = jnp.round(whole * np.float32(1 / 256)) * np.float32(256)
            cwide[slot, core, b, :K, :] = coarse.astype(jnp.bfloat16)
            cwide[slot, core, b, K:, :] = (whole - coarse).astype(jnp.bfloat16)

    widen(0, c)
    for slot in range(1, NJ):
        c_copies[slot - 1].wait_recv()
        pass_on(slot).start()
        widen(slot, c)
    bytes_of(cbuf.at[:, c1], recv_sem.at[2], False)
    for slot in range(NJ):
        widen(slot, c1)

    bytes_of(zbuf, recv_sem.at[3], False)
    z = zbuf[...].reshape(2 * GS * SLICE, NB * F)
    pre = jnp.dot(jnp.concatenate([z, z], axis=1), wbuf[...], preferred_element_type=jnp.float32)
    basis = jnp.tanh(pre + offsets).astype(jnp.bfloat16)
    twice = [jnp.concatenate([basis[:, b * K : (b + 1) * K]] * 2, axis=1) for b in range(NB)]

    for slot in range(NJ - 1, -1, -1):
        for b in range(NB):
            both = jnp.concatenate([cwide[slot, 0, b], cwide[slot, 1, b]], axis=1)
            values = jnp.dot(twice[b], both, preferred_element_type=jnp.float32)
            positive = jnp.sum(jnp.maximum(values, 0.0), axis=0, keepdims=True)
            part[slot, 0, b : b + 1, :] = positive[:, :SETS]
            part[slot, 1, b : b + 1, :] = positive[:, SETS:]
        for tc, tp in ((c1, p1), (c, p1), (c1, p), (c, p))[: 4 if slot else 3]:
            pltpu.make_async_remote_copy(
                src_ref=part.at[slot, tc], dst_ref=fin.at[slot * 4 + c * 2 + p], send_sem=send_sem.at[4], recv_sem=recv_sem.at[4],
                device_id={"trade": valued(slot) - c + tc, "path": tp}, device_id_type=MESH,
            ).start()

    fin[c * 2 + p] = part[0, c]
    bytes_of(fin.at[pl.ds(0, 15)], recv_sem.at[4], False)
    out[...] = jnp.sum(fin[...], axis=0) * unit[...] * np.float32(1.0 / (GS * SLICE * 32))

    bytes_of(nt, send_sem.at[0], True)
    bytes_of(cbuf.at[pl.ds(0, NJ - 1), c], send_sem.at[1], True)
    bytes_of(cbuf.at[:, c], send_sem.at[2], True)
    bytes_of(zbuf, send_sem.at[3], True)
    bytes_of(fin.at[pl.ds(0, 15)], send_sem.at[4], True)

    @pl.when(g == 0)
    def _():
        total_copy(1, 0).wait_send()

    @pl.when(g < 2)
    def _():
        total_copy(1, 1).wait_send()

    @pl.when(jnp.logical_not(outer))
    def _():
        bytes_of(nt, send_sem.at[5], True)


def shards(normals, chol, volatility, start_state, basis_map, basis_bias, coef, maturity, netting):
    args = (
        normals, chol, volatility.reshape(1, -1), start_state.reshape(1, -1), basis_map,
        basis_bias.reshape(1, -1), coef, maturity.reshape(1, -1), netting.reshape(1, -1),
    )
    args = [pltpu.with_memory_space_constraint(a, pltpu.HBM) for a in args]
    return pl.pallas_call(
        kernel,
        out_shape=jax.ShapeDtypeStruct((NB, SETS), jnp.float32),
        in_specs=[pl.BlockSpec(memory_space=pltpu.HBM)] * len(args),
        out_specs=pl.BlockSpec(memory_space=pltpu.VMEM),
        scratch_shapes=[pltpu.VMEM(a.shape, a.dtype) for a in args]
        + [
            pltpu.VMEM((GS, SLICE, NB * F), jnp.bfloat16),
            pltpu.VMEM((GS, SLICE, NB * F), jnp.bfloat16),
            pltpu.VMEM((GS, SLICE, NB * F), jnp.bfloat16),
            pltpu.VMEM((2, SLICE, NB * F), jnp.bfloat16),
            pltpu.VMEM((SLICE, NB * F), jnp.bfloat16),
            pltpu.VMEM((SLICE, NB * F), jnp.float32),
            pltpu.VMEM((GS, SLICE, NB * F), jnp.bfloat16),
            pltpu.VMEM((2 * GS, SLICE, NB * F), jnp.bfloat16),
            pltpu.VMEM((NJ, 2, NB, K, SETS), jnp.int16),
            pltpu.VMEM((NJ, 2, NB, 2 * K, SETS), jnp.bfloat16),
            pltpu.VMEM((NB, SETS), jnp.float32),
            pltpu.VMEM((2 * NB * F, NB * K), jnp.bfloat16),
            pltpu.VMEM((NJ, 2, NB, SETS), jnp.float32),
            pltpu.VMEM((16, NB, SETS), jnp.float32),
            pltpu.SemaphoreType.DMA((len(args),)),
            pltpu.SemaphoreType.DMA((6,)),
            pltpu.SemaphoreType.DMA((6,)),
            pltpu.SemaphoreType.DMA((NJ - 1,)),
            pltpu.SemaphoreType.DMA((1,)),
            pltpu.SemaphoreType.DMA((2,)),
            pltpu.SemaphoreType.REGULAR((2,)),
        ],
        compiler_params=pltpu.CompilerParams(
            collective_id=0, has_side_effects=True, vmem_limit_bytes=24 << 20
        ),
    )(*args)


def solution(mesh):
    placed = (
        P("date", None, ("trade", "path")),
        P(),
        P(),
        P(),
        P(),
        P(),
        P(None, "trade"),
        P("trade"),
        P("trade"),
    )
    return jax.shard_map(
        shards, mesh=mesh, in_specs=placed, out_specs=P("date", "trade"), check_vma=False
    )
```

```python
import jax
import jax.numpy as jnp
import numpy as np
from jax import lax
from jax.experimental import pallas as pl
from jax.experimental.pallas import tpu as pltpu
from jax.sharding import PartitionSpec as P

MESH = pl.DeviceIdType.MESH
ND = 16
NB = 2
F = 64
K = 128
SETS = 128
GS = 4
SLICE = 64
TOP = 127 * 256
NJ = 4
HIGH = lax.Precision.HIGHEST


def kernel(
    normals, chol, vol, start, bmap, bias, coef, mat, net,
    out,
    v_norm, v_chol, v_vol, v_start, v_bmap, v_bias, v_coef, v_mat, v_net,
    nt, arrived, ahead, tmsg, tbuf, base, sums, zbuf, cbuf, cwide, unit, wbuf, part, fin,
    load_sem, send_sem, recv_sem, c_sem, t_sem, t_sent, ready,
):
    d, t, p = lax.axis_index("date"), lax.axis_index("trade"), lax.axis_index("path")
    y, c = lax.div(t, 2), lax.rem(t, 2)
    par = lax.rem(y, 2)
    side = 2 * par - 1
    g, w = lax.div(d, GS), lax.rem(d, GS)
    c1, p1 = 1 - c, 1 - p
    twin = t - 2 * side

    def row(steps):
        return lax.rem(t + 2 * steps + 16, 16)

    def valued(slot):
        return row(side * slot)

    def valuer(slot):
        return row(side * slot * (1 if slot % 2 else -1))

    barrier = pltpu.get_barrier_semaphore()

    def hello(where):
        pl.semaphore_signal(barrier, inc=1, device_id=where, device_id_type=MESH)

    def mate(i):
        return {"date": g * GS + lax.rem(w + i, GS), "path": p1}

    def counterpart(group):
        return {"date": group * GS + w}

    for i in range(GS):
        hello(mate(i))
    for i in (1, 2, 3, -2):
        hello({"trade": row(side * i)})
    hello({"trade": twin})
    other = t + 1 - 2 * c
    hello({"trade": other})
    hello({"trade": other, "path": p1})

    @pl.when(g == 0)
    def _():
        hello(counterpart(1))
        hello(counterpart(3))

    @pl.when(g == 1)
    def _():
        hello(counterpart(2))

    outer = jnp.logical_or(g == 0, g == 3)
    beside = jnp.where(g < 2, 1 - g, 5 - g)

    def across(i):
        return {"date": beside * GS + lax.rem(w + i, GS), "path": p1}

    @pl.when(outer)
    def _():
        for i in range(GS):
            hello(across(i))

    loads = [
        pltpu.make_async_copy(a, b, load_sem.at[i])
        for i, (a, b) in enumerate(
            (
                (normals, v_norm), (coef, v_coef), (mat, v_mat), (net, v_net), (chol, v_chol),
                (vol, v_vol), (start, v_start), (bmap, v_bmap), (bias, v_bias),
            )
        )
    ]
    for load in loads:
        load.start()

    loads[0].wait()
    flat = v_norm[...].reshape(NB * F, GS * SLICE).astype(jnp.float32)
    nt[...] = flat.T.astype(jnp.bfloat16).reshape(GS, SLICE, NB * F)

    heard = jnp.where(g == 0, 0, 1) + jnp.where(outer, 0, GS)
    pl.semaphore_wait(barrier, GS + 4 + 3 + heard)

    for i in (2, 3, 1, 0):
        pltpu.make_async_remote_copy(
            src_ref=nt.at[lax.rem(w + i, GS)], dst_ref=arrived.at[w], send_sem=send_sem.at[0], recv_sem=recv_sem.at[0],
            device_id=mate(i), device_id_type=MESH,
        ).start()

    @pl.when(jnp.logical_not(outer))
    def _():
        for i in range(GS):
            pltpu.make_async_remote_copy(
                src_ref=nt.at[lax.rem(w + i, GS)], dst_ref=ahead.at[w], send_sem=send_sem.at[5], recv_sem=recv_sem.at[5],
                device_id=across(i), device_id_type=MESH,
            ).start()

    def say_ready(to, slot):
        pl.semaphore_signal(ready.at[slot], inc=1, device_id=counterpart(to), device_id_type=MESH)

    @pl.when(g == 1)
    def _():
        say_ready(0, 0)

    @pl.when(g == 2)
    def _():
        say_ready(1, 0)

    @pl.when(g == 3)
    def _():
        say_ready(0, 1)

    for load in loads[1:4]:
        load.wait()
    local_set = v_net[...] - t * SETS
    trades = v_coef.shape[1]
    member = (lax.broadcasted_iota(jnp.int32, (SETS, trades), 0) == local_set)
    member = member.astype(jnp.float32).astype(jnp.bfloat16)
    for b in range(NB):
        alive = (d * NB + b < v_mat[...]).astype(jnp.float32).astype(jnp.bfloat16)
        folded = lax.dot_general(
            v_coef[...] * alive, member, (((1,), (1,)), ((), ())), preferred_element_type=jnp.float32
        )
        largest = jnp.maximum(jnp.max(jnp.abs(folded), axis=0, keepdims=True), np.float32(1e-30))
        unit[b : b + 1, :] = largest * np.float32(1.0 / TOP)
        cbuf[0, c, b] = jnp.round(folded * (np.float32(TOP) / largest)).astype(jnp.int32).astype(jnp.int16)

    c_copies = [
        pltpu.make_async_remote_copy(
            src_ref=cbuf.at[0, c], dst_ref=cbuf.at[i, c], send_sem=send_sem.at[1], recv_sem=c_sem.at[i - 1],
            device_id={"trade": valuer(i)}, device_id_type=MESH,
        )
        for i in range(1, NJ)
    ]
    for copy in c_copies:
        copy.start()

    def pass_on(slot):
        return pltpu.make_async_remote_copy(
            src_ref=cbuf.at[slot, c], dst_ref=cbuf.at[slot, c], send_sem=send_sem.at[2], recv_sem=recv_sem.at[2],
            device_id={"trade": other}, device_id_type=MESH,
        )

    pass_on(0).start()

    for load in loads[4:]:
        load.wait()
    scale = v_vol[...] * np.float32(np.sqrt(np.float32(1.0) / np.float32(ND * NB)))
    joint = jnp.dot(v_chol[...].T * scale, v_bmap[...], precision=HIGH, preferred_element_type=jnp.float32)
    offset = jnp.dot(v_start[...], v_bmap[...], precision=HIGH, preferred_element_type=jnp.float32) + v_bias[...]
    joint_high = joint.astype(jnp.bfloat16)
    joint_low = (joint - joint_high.astype(jnp.float32)).astype(jnp.bfloat16)
    wbuf[...] = jnp.zeros_like(wbuf)
    for b in range(NB):
        wbuf[pl.ds(b * F, F), pl.ds(b * K, K)] = joint_high
        wbuf[pl.ds(NB * F + b * F, F), pl.ds(b * K, K)] = joint_low
    offsets = jnp.concatenate([offset, offset], axis=1)

    def bytes_of(ref, sem, send):
        whole = pltpu.make_async_remote_copy(
            src_ref=ref, dst_ref=ref, send_sem=sem, recv_sem=sem, device_id={"trade": other}, device_id_type=MESH
        )
        return whole.wait_send() if send else whole.wait_recv()

    bytes_of(arrived, recv_sem.at[0], False)
    later_half = lax.broadcasted_iota(jnp.int32, (SLICE, NB * F), 1) >= F

    def twofold(message):
        message = message.astype(jnp.float32)
        return message + pltpu.roll(message, F, axis=1)

    def terms(value):
        high = value.astype(jnp.bfloat16).astype(jnp.float32)
        return jnp.where(later_half, value - high, value).astype(jnp.bfloat16)

    blocks = [arrived[e].astype(jnp.float32) for e in range(GS)]
    pairs = [block + pltpu.roll(block, F, axis=1) for block in blocks]
    own = pairs[0] + pairs[1] + pairs[2] + pairs[3]
    tmsg[0] = terms(own)

    def total_copy(to, message):
        return pltpu.make_async_remote_copy(
            src_ref=tmsg.at[message], dst_ref=tbuf, send_sem=t_sent.at[message], recv_sem=t_sem.at[0],
            device_id=counterpart(to), device_id_type=MESH,
        )

    @pl.when(g == 0)
    def _():
        base[...] = jnp.zeros_like(base)
        pl.semaphore_wait(ready.at[0], 1)
        total_copy(1, 0).start()

    @pl.when(g > 0)
    def _():
        total_copy(0, 0).wait_recv()
        base[...] = twofold(tbuf[...])

    @pl.when(g == 1)
    def _():
        tmsg[1] = terms(own + base[...])
        pl.semaphore_wait(ready.at[0], 1)
        total_copy(2, 1).start()

    @pl.when(g == 3)
    def _():
        bytes_of(ahead, recv_sem.at[5], False)
        base[...] += sum(twofold(ahead[e]) for e in range(GS))

    total = base[...]
    for e in range(GS):
        sums[e] = (total + jnp.where(later_half, pairs[e], blocks[e])).astype(jnp.bfloat16)
        total = total + pairs[e]
        for where in (twin, t):
            pltpu.make_async_remote_copy(
                src_ref=sums.at[e], dst_ref=zbuf.at[par * GS + w], send_sem=send_sem.at[3], recv_sem=recv_sem.at[3],
                device_id={"date": g * GS + e, "path": p1, "trade": where}, device_id_type=MESH,
            ).start()

    @pl.when(g == 0)
    def _():
        bytes_of(ahead, recv_sem.at[5], False)
        tmsg[1] = terms(own + sum(twofold(ahead[e]) for e in range(GS)))
        pl.semaphore_wait(ready.at[1], 1)
        total_copy(3, 1).start()

    def widen(slot, core):
        for b in range(NB):
            whole = cbuf[slot, core, b].astype(jnp.int32).astype(jnp.float32)
            coarse = jnp.round(whole * np.float32(1 / 256)) * np.float32(256)
            cwide[slot, core, b, :K, :] = coarse.astype(jnp.bfloat16)
            cwide[slot, core, b, K:, :] = (whole - coarse).astype(jnp.bfloat16)

    widen(0, c)
    for slot in range(1, NJ):
        c_copies[slot - 1].wait_recv()
        pass_on(slot).start()
        widen(slot, c)
    bytes_of(cbuf.at[:, c1], recv_sem.at[2], False)
    for slot in range(NJ):
        widen(slot, c1)

    bytes_of(zbuf, recv_sem.at[3], False)
    z = zbuf[...].reshape(2 * GS * SLICE, NB * F)
    pre = jnp.dot(jnp.concatenate([z, z], axis=1), wbuf[...], preferred_element_type=jnp.float32)
    basis = jnp.tanh(pre + offsets).astype(jnp.bfloat16)
    twice = [jnp.concatenate([basis[:, b * K : (b + 1) * K]] * 2, axis=1) for b in range(NB)]

    for slot in range(NJ - 1, -1, -1):
        for b in range(NB):
            both = jnp.concatenate([cwide[slot, 0, b], cwide[slot, 1, b]], axis=1)
            values = jnp.dot(twice[b], both, preferred_element_type=jnp.float32)
            positive = jnp.sum(jnp.maximum(values, 0.0), axis=0, keepdims=True)
            part[slot, 0, b : b + 1, :] = positive[:, :SETS]
            part[slot, 1, b : b + 1, :] = positive[:, SETS:]
        for tc, tp in ((c1, p1), (c, p1), (c1, p), (c, p))[: 4 if slot else 3]:
            pltpu.make_async_remote_copy(
                src_ref=part.at[slot, tc], dst_ref=fin.at[slot * 4 + c * 2 + p], send_sem=send_sem.at[4], recv_sem=recv_sem.at[4],
                device_id={"trade": valued(slot) - c + tc, "path": tp}, device_id_type=MESH,
            ).start()

    fin[c * 2 + p] = part[0, c]
    bytes_of(fin.at[pl.ds(0, 15)], recv_sem.at[4], False)
    out[...] = jnp.sum(fin[...], axis=0) * unit[...] * np.float32(1.0 / (GS * SLICE * 32))

    bytes_of(nt, send_sem.at[0], True)
    bytes_of(cbuf.at[pl.ds(0, NJ - 1), c], send_sem.at[1], True)
    bytes_of(cbuf.at[:, c], send_sem.at[2], True)
    bytes_of(zbuf, send_sem.at[3], True)
    bytes_of(fin.at[pl.ds(0, 15)], send_sem.at[4], True)

    @pl.when(g == 0)
    def _():
        total_copy(1, 0).wait_send()

    @pl.when(g < 2)
    def _():
        total_copy(1, 1).wait_send()

    @pl.when(jnp.logical_not(outer))
    def _():
        bytes_of(nt, send_sem.at[5], True)


def shards(normals, chol, volatility, start_state, basis_map, basis_bias, coef, maturity, netting):
    args = (
        normals, chol, volatility.reshape(1, -1), start_state.reshape(1, -1), basis_map,
        basis_bias.reshape(1, -1), coef, maturity.reshape(1, -1), netting.reshape(1, -1),
    )
    args = [pltpu.with_memory_space_constraint(a, pltpu.HBM) for a in args]
    return pl.pallas_call(
        kernel,
        out_shape=jax.ShapeDtypeStruct((NB, SETS), jnp.float32),
        in_specs=[pl.BlockSpec(memory_space=pltpu.HBM)] * len(args),
        out_specs=pl.BlockSpec(memory_space=pltpu.VMEM),
        scratch_shapes=[pltpu.VMEM(a.shape, a.dtype) for a in args]
        + [
            pltpu.VMEM((GS, SLICE, NB * F), jnp.bfloat16),
            pltpu.VMEM((GS, SLICE, NB * F), jnp.bfloat16),
            pltpu.VMEM((GS, SLICE, NB * F), jnp.bfloat16),
            pltpu.VMEM((2, SLICE, NB * F), jnp.bfloat16),
            pltpu.VMEM((SLICE, NB * F), jnp.bfloat16),
            pltpu.VMEM((SLICE, NB * F), jnp.float32),
            pltpu.VMEM((GS, SLICE, NB * F), jnp.bfloat16),
            pltpu.VMEM((2 * GS, SLICE, NB * F), jnp.bfloat16),
            pltpu.VMEM((NJ, 2, NB, K, SETS), jnp.int16),
            pltpu.VMEM((NJ, 2, NB, 2 * K, SETS), jnp.bfloat16),
            pltpu.VMEM((NB, SETS), jnp.float32),
            pltpu.VMEM((2 * NB * F, NB * K), jnp.bfloat16),
            pltpu.VMEM((NJ, 2, NB, SETS), jnp.float32),
            pltpu.VMEM((16, NB, SETS), jnp.float32),
            pltpu.SemaphoreType.DMA((len(args),)),
            pltpu.SemaphoreType.DMA((6,)),
            pltpu.SemaphoreType.DMA((6,)),
            pltpu.SemaphoreType.DMA((NJ - 1,)),
            pltpu.SemaphoreType.DMA((1,)),
            pltpu.SemaphoreType.DMA((2,)),
            pltpu.SemaphoreType.REGULAR((2,)),
        ],
        compiler_params=pltpu.CompilerParams(
            collective_id=0, has_side_effects=True, vmem_limit_bytes=24 << 20
        ),
    )(*args)


def solution(mesh):
    placed = (
        P("date", None, ("trade", "path")),
        P(),
        P(),
        P(),
        P(),
        P(),
        P(None, "trade"),
        P("trade"),
        P("trade"),
    )
    return jax.shard_map(
        shards, mesh=mesh, in_specs=placed, out_specs=P("date", "trade"), check_vma=False
    )
```

```python
import jax
import jax.numpy as jnp
import numpy as np
from jax import lax
from jax.experimental import pallas as pl
from jax.experimental.pallas import tpu as pltpu
from jax.sharding import PartitionSpec as P

MESH = pl.DeviceIdType.MESH
ND = 16
NB = 2
F = 64
K = 128
SETS = 128
GS = 4
SLICE = 64
HALF = SLICE // 2
PATHS = GS * SLICE
TOP = 127 * 256
NJ = 4
HIGH = lax.Precision.HIGHEST


def kernel(
    normals, chol, vol, start, bmap, bias, coef, mat, net,
    out,
    v_norm, v_chol, v_vol, v_start, v_bmap, v_bias, v_coef, v_mat, v_net,
    own_n, near_n, local, slices, arrived, ahead, tmsg, tbuf, base, sums, zbuf, zrows, cbuf, cwide, unit, wbuf, part, fin,
    load_sem, send_sem, recv_sem, c_sem, t_sem, t_sent, ready,
):
    d, t, p = lax.axis_index("date"), lax.axis_index("trade"), lax.axis_index("path")
    y, c = lax.div(t, 2), lax.rem(t, 2)
    par = lax.rem(y, 2)
    side = 2 * par - 1
    g, w = lax.div(d, GS), lax.rem(d, GS)
    c1, p1 = 1 - c, 1 - p
    twin = t - 2 * side

    def row(steps):
        return lax.rem(t + 2 * steps + 16, 16)

    def valued(slot):
        return row(side * slot)

    def valuer(slot):
        return row(side * slot * (1 if slot % 2 else -1))

    barrier = pltpu.get_barrier_semaphore()

    def hello(where):
        pl.semaphore_signal(barrier, inc=1, device_id=where, device_id_type=MESH)

    def mate(i):
        return {"date": g * GS + lax.rem(w + i, GS), "path": p1}

    def counterpart(group):
        return {"date": group * GS + w}

    for i in range(GS):
        hello(mate(i))
    for i in (1, 2, 3, -2):
        hello({"trade": row(side * i)})
    hello({"trade": twin})
    other = t + 1 - 2 * c
    hello({"trade": other})
    hello({"trade": other, "path": p1})

    @pl.when(g == 0)
    def _():
        hello(counterpart(1))
        hello(counterpart(3))

    @pl.when(g == 1)
    def _():
        hello(counterpart(2))

    outer = jnp.logical_or(g == 0, g == 3)
    beside = jnp.where(g < 2, 1 - g, 5 - g)

    def across(i):
        return {"date": beside * GS + lax.rem(w + i, GS), "path": p1}

    @pl.when(outer)
    def _():
        for i in range(GS):
            hello(across(i))

    loads = [
        pltpu.make_async_copy(a, b, load_sem.at[i])
        for i, (a, b) in enumerate(
            (
                (normals, v_norm), (coef, v_coef), (mat, v_mat), (net, v_net), (chol, v_chol),
                (vol, v_vol), (start, v_start), (bmap, v_bmap), (bias, v_bias),
            )
        )
    ]
    for load in loads:
        load.start()

    def odd_half(rows):
        return lax.broadcasted_iota(jnp.int32, (rows, NB * F), 1) >= F

    def swapped(block):
        return pltpu.roll(block, F, axis=1)

    loads[0].wait()
    normal = v_norm[...].reshape(NB * F, PATHS).astype(jnp.float32).T
    both = normal + swapped(normal)
    for i in range(GS):
        first = i * SLICE
        slices[i] = jnp.where(
            odd_half(HALF), both[first + HALF : first + SLICE], both[first : first + HALF]
        ).astype(jnp.bfloat16)

    heard = jnp.where(g == 0, 0, 1) + jnp.where(outer, 0, GS)
    pl.semaphore_wait(barrier, GS + 4 + 3 + heard)

    for i in (2, 3, 1, 0):
        pltpu.make_async_remote_copy(
            src_ref=slices.at[lax.rem(w + i, GS)], dst_ref=arrived.at[w], send_sem=send_sem.at[0], recv_sem=recv_sem.at[0],
            device_id=mate(i), device_id_type=MESH,
        ).start()

    @pl.when(jnp.logical_not(outer))
    def _():
        for i in range(GS):
            pltpu.make_async_remote_copy(
                src_ref=slices.at[lax.rem(w + i, GS)], dst_ref=ahead.at[w], send_sem=send_sem.at[5], recv_sem=recv_sem.at[5],
                device_id=across(i), device_id_type=MESH,
            ).start()

    def say_ready(to, slot):
        pl.semaphore_signal(ready.at[slot], inc=1, device_id=counterpart(to), device_id_type=MESH)

    @pl.when(g == 1)
    def _():
        say_ready(0, 0)

    @pl.when(g == 2)
    def _():
        say_ready(1, 0)

    @pl.when(g == 3)
    def _():
        say_ready(0, 1)

    own_n[...] = normal.astype(jnp.bfloat16)
    neighbour = pltpu.make_async_remote_copy(
        src_ref=own_n, dst_ref=near_n, send_sem=send_sem.at[6], recv_sem=recv_sem.at[6],
        device_id={"trade": twin}, device_id_type=MESH,
    )
    neighbour.start()
    local[par] = jnp.where(odd_half(PATHS), both, normal)

    for load in loads[1:4]:
        load.wait()
    local_set = v_net[...] - t * SETS
    trades = v_coef.shape[1]
    member = (lax.broadcasted_iota(jnp.int32, (SETS, trades), 0) == local_set)
    member = member.astype(jnp.float32).astype(jnp.bfloat16)
    for b in range(NB):
        alive = (d * NB + b < v_mat[...]).astype(jnp.float32).astype(jnp.bfloat16)
        folded = lax.dot_general(
            v_coef[...] * alive, member, (((1,), (1,)), ((), ())), preferred_element_type=jnp.float32
        )
        largest = jnp.maximum(jnp.max(jnp.abs(folded), axis=0, keepdims=True), np.float32(1e-30))
        unit[b : b + 1, :] = largest * np.float32(1.0 / TOP)
        cbuf[0, c, b] = jnp.round(folded * (np.float32(TOP) / largest)).astype(jnp.int32).astype(jnp.int16)

    c_copies = [
        pltpu.make_async_remote_copy(
            src_ref=cbuf.at[0, c], dst_ref=cbuf.at[i, c], send_sem=send_sem.at[1], recv_sem=c_sem.at[i - 1],
            device_id={"trade": valuer(i)}, device_id_type=MESH,
        )
        for i in range(1, NJ)
    ]
    for copy in c_copies:
        copy.start()

    def pass_on(slot):
        return pltpu.make_async_remote_copy(
            src_ref=cbuf.at[slot, c], dst_ref=cbuf.at[slot, c], send_sem=send_sem.at[2], recv_sem=recv_sem.at[2],
            device_id={"trade": other}, device_id_type=MESH,
        )

    pass_on(0).start()

    for load in loads[4:]:
        load.wait()
    scale = v_vol[...] * np.float32(np.sqrt(np.float32(1.0) / np.float32(ND * NB)))
    joint = jnp.dot(v_chol[...].T * scale, v_bmap[...], precision=HIGH, preferred_element_type=jnp.float32)
    offset = jnp.dot(v_start[...], v_bmap[...], precision=HIGH, preferred_element_type=jnp.float32) + v_bias[...]
    joint_high = joint.astype(jnp.bfloat16)
    joint_low = (joint - joint_high.astype(jnp.float32)).astype(jnp.bfloat16)
    wbuf[...] = jnp.zeros_like(wbuf)
    for b in range(NB):
        wbuf[pl.ds(b * F, F), pl.ds(b * K, K)] = joint_high
        wbuf[pl.ds(NB * F + b * F, F), pl.ds(b * K, K)] = joint_low
    offsets = jnp.concatenate([offset, offset], axis=1)

    def bytes_of(ref, sem, send):
        whole = pltpu.make_async_remote_copy(
            src_ref=ref, dst_ref=ref, send_sem=sem, recv_sem=sem, device_id={"trade": other}, device_id_type=MESH
        )
        return whole.wait_send() if send else whole.wait_recv()

    bytes_of(arrived, recv_sem.at[0], False)
    blocks = [arrived[e].astype(jnp.float32) for e in range(GS)]
    own = blocks[0] + blocks[1] + blocks[2] + blocks[3]
    tmsg[0] = own.astype(jnp.bfloat16)

    def total_copy(to, message):
        return pltpu.make_async_remote_copy(
            src_ref=tmsg.at[message], dst_ref=tbuf, send_sem=t_sent.at[message], recv_sem=t_sem.at[0],
            device_id=counterpart(to), device_id_type=MESH,
        )

    @pl.when(g == 0)
    def _():
        base[...] = jnp.zeros_like(base)
        pl.semaphore_wait(ready.at[0], 1)
        total_copy(1, 0).start()

    @pl.when(g > 0)
    def _():
        total_copy(0, 0).wait_recv()
        base[...] = tbuf[...].astype(jnp.float32)

    @pl.when(g == 1)
    def _():
        tmsg[1] = (own + base[...]).astype(jnp.bfloat16)
        pl.semaphore_wait(ready.at[0], 1)
        total_copy(2, 1).start()

    @pl.when(g == 3)
    def _():
        bytes_of(ahead, recv_sem.at[5], False)
        base[...] += sum(ahead[e].astype(jnp.float32) for e in range(GS))

    total = base[...]
    for e in range(GS):
        sums[e] = total.astype(jnp.bfloat16)
        total = total + blocks[e]
        for where in (twin, t):
            pltpu.make_async_remote_copy(
                src_ref=sums.at[e], dst_ref=zbuf.at[par * GS + w], send_sem=send_sem.at[3], recv_sem=recv_sem.at[3],
                device_id={"date": g * GS + e, "path": p1, "trade": where}, device_id_type=MESH,
            ).start()

    @pl.when(g == 0)
    def _():
        bytes_of(ahead, recv_sem.at[5], False)
        tmsg[1] = (own + sum(ahead[e].astype(jnp.float32) for e in range(GS))).astype(jnp.bfloat16)
        pl.semaphore_wait(ready.at[1], 1)
        total_copy(3, 1).start()

    neighbour.wait_recv()
    normal = near_n[...].astype(jnp.float32)
    local[1 - par] = normal + jnp.where(odd_half(PATHS), swapped(normal), 0.0)

    def widen(slot, core):
        for b in range(NB):
            whole = cbuf[slot, core, b].astype(jnp.int32).astype(jnp.float32)
            coarse = jnp.round(whole * np.float32(1 / 256)) * np.float32(256)
            cwide[slot, core, b, :K, :] = coarse.astype(jnp.bfloat16)
            cwide[slot, core, b, K:, :] = (whole - coarse).astype(jnp.bfloat16)

    widen(0, c)
    for slot in range(1, NJ):
        c_copies[slot - 1].wait_recv()
        pass_on(slot).start()
        widen(slot, c)
    bytes_of(cbuf.at[:, c1], recv_sem.at[2], False)
    for slot in range(NJ):
        widen(slot, c1)

    bytes_of(zbuf, recv_sem.at[3], False)
    for half in range(2):
        for i in range(GS):
            before = zbuf[half * GS + i].astype(jnp.float32)
            across_lanes = swapped(before)
            rows = pl.ds(i * SLICE, HALF)
            zrows[half, rows] = (local[half, rows] + jnp.where(odd_half(HALF), across_lanes, before)).astype(jnp.bfloat16)
            rows = pl.ds(i * SLICE + HALF, HALF)
            zrows[half, rows] = (local[half, rows] + jnp.where(odd_half(HALF), before, across_lanes)).astype(jnp.bfloat16)
    z = zrows[...].reshape(2 * PATHS, NB * F)
    pre = jnp.dot(jnp.concatenate([z, z], axis=1), wbuf[...], preferred_element_type=jnp.float32)
    basis = jnp.tanh(pre + offsets).astype(jnp.bfloat16)
    twice = [jnp.concatenate([basis[:, b * K : (b + 1) * K]] * 2, axis=1) for b in range(NB)]

    for slot in range(NJ - 1, -1, -1):
        for b in range(NB):
            both = jnp.concatenate([cwide[slot, 0, b], cwide[slot, 1, b]], axis=1)
            values = jnp.dot(twice[b], both, preferred_element_type=jnp.float32)
            positive = jnp.sum(jnp.maximum(values, 0.0), axis=0, keepdims=True)
            part[slot, 0, b : b + 1, :] = positive[:, :SETS]
            part[slot, 1, b : b + 1, :] = positive[:, SETS:]
        for tc, tp in ((c1, p1), (c, p1), (c1, p), (c, p))[: 4 if slot else 3]:
            pltpu.make_async_remote_copy(
                src_ref=part.at[slot, tc], dst_ref=fin.at[slot * 4 + c * 2 + p], send_sem=send_sem.at[4], recv_sem=recv_sem.at[4],
                device_id={"trade": valued(slot) - c + tc, "path": tp}, device_id_type=MESH,
            ).start()

    fin[c * 2 + p] = part[0, c]
    bytes_of(fin.at[pl.ds(0, 15)], recv_sem.at[4], False)
    out[...] = jnp.sum(fin[...], axis=0) * unit[...] * np.float32(1.0 / (PATHS * 32))

    bytes_of(slices, send_sem.at[0], True)
    neighbour.wait_send()
    bytes_of(cbuf.at[pl.ds(0, NJ - 1), c], send_sem.at[1], True)
    bytes_of(cbuf.at[:, c], send_sem.at[2], True)
    bytes_of(zbuf, send_sem.at[3], True)
    bytes_of(fin.at[pl.ds(0, 15)], send_sem.at[4], True)

    @pl.when(g == 0)
    def _():
        total_copy(1, 0).wait_send()

    @pl.when(g < 2)
    def _():
        total_copy(1, 1).wait_send()

    @pl.when(jnp.logical_not(outer))
    def _():
        bytes_of(slices, send_sem.at[5], True)


def shards(normals, chol, volatility, start_state, basis_map, basis_bias, coef, maturity, netting):
    args = (
        normals, chol, volatility.reshape(1, -1), start_state.reshape(1, -1), basis_map,
        basis_bias.reshape(1, -1), coef, maturity.reshape(1, -1), netting.reshape(1, -1),
    )
    args = [pltpu.with_memory_space_constraint(a, pltpu.HBM) for a in args]
    return pl.pallas_call(
        kernel,
        out_shape=jax.ShapeDtypeStruct((NB, SETS), jnp.float32),
        in_specs=[pl.BlockSpec(memory_space=pltpu.HBM)] * len(args),
        out_specs=pl.BlockSpec(memory_space=pltpu.VMEM),
        scratch_shapes=[pltpu.VMEM(a.shape, a.dtype) for a in args]
        + [
            pltpu.VMEM((PATHS, NB * F), jnp.bfloat16),
            pltpu.VMEM((PATHS, NB * F), jnp.bfloat16),
            pltpu.VMEM((2, PATHS, NB * F), jnp.float32),
            pltpu.VMEM((GS, HALF, NB * F), jnp.bfloat16),
            pltpu.VMEM((GS, HALF, NB * F), jnp.bfloat16),
            pltpu.VMEM((GS, HALF, NB * F), jnp.bfloat16),
            pltpu.VMEM((2, HALF, NB * F), jnp.bfloat16),
            pltpu.VMEM((HALF, NB * F), jnp.bfloat16),
            pltpu.VMEM((HALF, NB * F), jnp.float32),
            pltpu.VMEM((GS, HALF, NB * F), jnp.bfloat16),
            pltpu.VMEM((2 * GS, HALF, NB * F), jnp.bfloat16),
            pltpu.VMEM((2, PATHS, NB * F), jnp.bfloat16),
            pltpu.VMEM((NJ, 2, NB, K, SETS), jnp.int16),
            pltpu.VMEM((NJ, 2, NB, 2 * K, SETS), jnp.bfloat16),
            pltpu.VMEM((NB, SETS), jnp.float32),
            pltpu.VMEM((2 * NB * F, NB * K), jnp.bfloat16),
            pltpu.VMEM((NJ, 2, NB, SETS), jnp.float32),
            pltpu.VMEM((16, NB, SETS), jnp.float32),
            pltpu.SemaphoreType.DMA((len(args),)),
            pltpu.SemaphoreType.DMA((7,)),
            pltpu.SemaphoreType.DMA((7,)),
            pltpu.SemaphoreType.DMA((NJ - 1,)),
            pltpu.SemaphoreType.DMA((1,)),
            pltpu.SemaphoreType.DMA((2,)),
            pltpu.SemaphoreType.REGULAR((2,)),
        ],
        compiler_params=pltpu.CompilerParams(
            collective_id=0, has_side_effects=True, vmem_limit_bytes=24 << 20
        ),
    )(*args)


def solution(mesh):
    placed = (
        P("date", None, ("trade", "path")),
        P(),
        P(),
        P(),
        P(),
        P(),
        P(None, "trade"),
        P("trade"),
        P("trade"),
    )
    return jax.shard_map(
        shards, mesh=mesh, in_specs=placed, out_specs=P("date", "trade"), check_vma=False
    )
```

```python
import jax
import jax.numpy as jnp
import numpy as np
from jax import lax
from jax.experimental import pallas as pl
from jax.experimental.pallas import tpu as pltpu
from jax.sharding import PartitionSpec as P

MESH = pl.DeviceIdType.MESH
ND = 16
NB = 2
F = 64
K = 128
SETS = 128
GS = 4
SLICE = 64
HALF = SLICE // 2
PATHS = GS * SLICE
TOP = 127 * 256
NJ = 4
HIGH = lax.Precision.HIGHEST


def kernel(
    normals, chol, vol, start, bmap, bias, coef, mat, net,
    out,
    v_norm, v_chol, v_vol, v_start, v_bmap, v_bias, v_coef, v_mat, v_net,
    own_n, near_n, local, slices, arrived, ahead, tmsg, tbuf, base, sums, zbuf, tz, zrows, cbuf, cwide, unit, wbuf, part, fin,
    load_sem, send_sem, recv_sem, c_sem, t_sem, t_sent, ready,
):
    d, t, p = lax.axis_index("date"), lax.axis_index("trade"), lax.axis_index("path")
    y, c = lax.div(t, 2), lax.rem(t, 2)
    par = lax.rem(y, 2)
    side = 2 * par - 1
    g, w = lax.div(d, GS), lax.rem(d, GS)
    c1, p1 = 1 - c, 1 - p
    twin = t - 2 * side

    def row(steps):
        return lax.rem(t + 2 * steps + 16, 16)

    def valued(slot):
        return row(side * slot)

    def valuer(slot):
        return row(side * slot * (1 if slot % 2 else -1))

    barrier = pltpu.get_barrier_semaphore()

    def hello(where):
        pl.semaphore_signal(barrier, inc=1, device_id=where, device_id_type=MESH)

    def mate(i):
        return {"date": g * GS + lax.rem(w + i, GS), "path": p1}

    def counterpart(group, where=t):
        return {"date": group * GS + w, "trade": where}

    for i in range(GS):
        hello(mate(i))
    for i in (1, 2, 3, -2):
        hello({"trade": row(side * i)})
    hello({"trade": twin})
    other = t + 1 - 2 * c
    hello({"trade": other})
    hello({"trade": other, "path": p1})

    @pl.when(g == 0)
    def _():
        hello(counterpart(1))
        hello(counterpart(3))

    @pl.when(g == 1)
    def _():
        hello(counterpart(2))
        hello(counterpart(2, twin))

    outer = jnp.logical_or(g == 0, g == 3)
    beside = jnp.where(g < 2, 1 - g, 5 - g)

    def across(i):
        return {"date": beside * GS + lax.rem(w + i, GS), "path": p1}

    @pl.when(outer)
    def _():
        for i in range(GS):
            hello(across(i))

    loads = [
        pltpu.make_async_copy(a, b, load_sem.at[i])
        for i, (a, b) in enumerate(
            (
                (normals, v_norm), (coef, v_coef), (mat, v_mat), (net, v_net), (chol, v_chol),
                (vol, v_vol), (start, v_start), (bmap, v_bmap), (bias, v_bias),
            )
        )
    ]
    for load in loads:
        load.start()

    def odd_half(rows):
        return lax.broadcasted_iota(jnp.int32, (rows, NB * F), 1) >= F

    def swapped(block):
        return pltpu.roll(block, F, axis=1)

    loads[0].wait()
    normal = v_norm[...].reshape(NB * F, PATHS).astype(jnp.float32).T
    both = normal + swapped(normal)
    for i in range(GS):
        first = i * SLICE
        slices[i] = jnp.where(
            odd_half(HALF), both[first + HALF : first + SLICE], both[first : first + HALF]
        ).astype(jnp.bfloat16)

    heard = jnp.where(g == 0, 0, 1) + jnp.where(g == 2, 1, 0) + jnp.where(outer, 0, GS)
    pl.semaphore_wait(barrier, GS + 4 + 3 + heard)

    for i in (2, 3, 1, 0):
        pltpu.make_async_remote_copy(
            src_ref=slices.at[lax.rem(w + i, GS)], dst_ref=arrived.at[w], send_sem=send_sem.at[0], recv_sem=recv_sem.at[0],
            device_id=mate(i), device_id_type=MESH,
        ).start()

    @pl.when(jnp.logical_not(outer))
    def _():
        for i in range(GS):
            pltpu.make_async_remote_copy(
                src_ref=slices.at[lax.rem(w + i, GS)], dst_ref=ahead.at[w], send_sem=send_sem.at[5], recv_sem=recv_sem.at[5],
                device_id=across(i), device_id_type=MESH,
            ).start()

    def say_ready(to, slot, where=t):
        pl.semaphore_signal(ready.at[slot], inc=1, device_id=counterpart(to, where), device_id_type=MESH)

    @pl.when(g == 1)
    def _():
        say_ready(0, 0)

    @pl.when(g == 2)
    def _():
        say_ready(1, 0)
        say_ready(1, 0, twin)

    @pl.when(g == 3)
    def _():
        say_ready(0, 1)

    own_n[...] = normal.astype(jnp.bfloat16)
    neighbour = pltpu.make_async_remote_copy(
        src_ref=own_n, dst_ref=near_n, send_sem=send_sem.at[6], recv_sem=recv_sem.at[6],
        device_id={"trade": twin}, device_id_type=MESH,
    )
    neighbour.start()
    local[par] = jnp.where(odd_half(PATHS), both, normal)

    for load in loads[1:4]:
        load.wait()
    local_set = v_net[...] - t * SETS
    trades = v_coef.shape[1]
    member = (lax.broadcasted_iota(jnp.int32, (SETS, trades), 0) == local_set)
    member = member.astype(jnp.float32).astype(jnp.bfloat16)
    for b in range(NB):
        alive = (d * NB + b < v_mat[...]).astype(jnp.float32).astype(jnp.bfloat16)
        folded = lax.dot_general(
            v_coef[...] * alive, member, (((1,), (1,)), ((), ())), preferred_element_type=jnp.float32
        )
        largest = jnp.maximum(jnp.max(jnp.abs(folded), axis=0, keepdims=True), np.float32(1e-30))
        unit[b : b + 1, :] = largest * np.float32(1.0 / TOP)
        cbuf[0, c, b] = jnp.round(folded * (np.float32(TOP) / largest)).astype(jnp.int32).astype(jnp.int16)

    c_copies = [
        pltpu.make_async_remote_copy(
            src_ref=cbuf.at[0, c], dst_ref=cbuf.at[i, c], send_sem=send_sem.at[1], recv_sem=c_sem.at[i - 1],
            device_id={"trade": valuer(i)}, device_id_type=MESH,
        )
        for i in range(1, NJ)
    ]
    for copy in c_copies:
        copy.start()

    def pass_on(slot):
        return pltpu.make_async_remote_copy(
            src_ref=cbuf.at[slot, c], dst_ref=cbuf.at[slot, c], send_sem=send_sem.at[2], recv_sem=recv_sem.at[2],
            device_id={"trade": other}, device_id_type=MESH,
        )

    pass_on(0).start()

    for load in loads[4:]:
        load.wait()
    scale = v_vol[...] * np.float32(np.sqrt(np.float32(1.0) / np.float32(ND * NB)))
    joint = jnp.dot(v_chol[...].T * scale, v_bmap[...], precision=HIGH, preferred_element_type=jnp.float32)
    offset = jnp.dot(v_start[...], v_bmap[...], precision=HIGH, preferred_element_type=jnp.float32) + v_bias[...]
    joint_high = joint.astype(jnp.bfloat16)
    joint_low = (joint - joint_high.astype(jnp.float32)).astype(jnp.bfloat16)
    wbuf[...] = jnp.zeros_like(wbuf)
    for b in range(NB):
        wbuf[pl.ds(b * F, F), pl.ds(b * K, K)] = joint_high
        wbuf[pl.ds(NB * F + b * F, F), pl.ds(b * K, K)] = joint_low
    offsets = jnp.concatenate([offset, offset], axis=1)

    def bytes_of(ref, sem, send):
        whole = pltpu.make_async_remote_copy(
            src_ref=ref, dst_ref=ref, send_sem=sem, recv_sem=sem, device_id={"trade": other}, device_id_type=MESH
        )
        return whole.wait_send() if send else whole.wait_recv()

    bytes_of(arrived, recv_sem.at[0], False)
    blocks = [arrived[e].astype(jnp.float32) for e in range(GS)]
    own = blocks[0] + blocks[1] + blocks[2] + blocks[3]
    tmsg[0] = own.astype(jnp.bfloat16)

    def total_copy(to, message):
        return pltpu.make_async_remote_copy(
            src_ref=tmsg.at[message], dst_ref=tbuf, send_sem=t_sent.at[message], recv_sem=t_sem.at[0],
            device_id=counterpart(to), device_id_type=MESH,
        )

    @pl.when(g == 0)
    def _():
        base[...] = jnp.zeros_like(base)
        pl.semaphore_wait(ready.at[0], 1)
        total_copy(1, 0).start()

    @pl.when(g == 2)
    def _():
        base[...] = jnp.zeros_like(base)

    @pl.when(jnp.logical_or(g == 1, g == 3))
    def _():
        total_copy(0, 0).wait_recv()
        base[...] = tbuf[...].astype(jnp.float32)

    @pl.when(g == 3)
    def _():
        bytes_of(ahead, recv_sem.at[5], False)
        base[...] += sum(ahead[e].astype(jnp.float32) for e in range(GS))

    total = base[...]
    for e in range(GS):
        sums[e] = total.astype(jnp.bfloat16)
        total = total + blocks[e]
        for where in (twin, t):
            pltpu.make_async_remote_copy(
                src_ref=sums.at[e], dst_ref=zbuf.at[par * GS + w], send_sem=send_sem.at[3], recv_sem=recv_sem.at[3],
                device_id={"date": g * GS + e, "path": p1, "trade": where}, device_id_type=MESH,
            ).start()

    @pl.when(g == 1)
    def _():
        tmsg[1] = (own + base[...]).astype(jnp.bfloat16)
        pl.semaphore_wait(ready.at[0], 2)
        for i in range(GS):
            for where in (twin, t):
                pltpu.make_async_remote_copy(
                    src_ref=tmsg.at[1], dst_ref=tz.at[par * GS + w], send_sem=t_sent.at[1], recv_sem=t_sem.at[1],
                    device_id={"date": 2 * GS + i, "path": p1, "trade": where}, device_id_type=MESH,
                ).start()

    @pl.when(g == 0)
    def _():
        bytes_of(ahead, recv_sem.at[5], False)
        tmsg[1] = (own + sum(ahead[e].astype(jnp.float32) for e in range(GS))).astype(jnp.bfloat16)
        pl.semaphore_wait(ready.at[1], 1)
        total_copy(3, 1).start()

    neighbour.wait_recv()
    normal = near_n[...].astype(jnp.float32)
    local[1 - par] = normal + jnp.where(odd_half(PATHS), swapped(normal), 0.0)

    def widen(slot, core):
        for b in range(NB):
            whole = cbuf[slot, core, b].astype(jnp.int32).astype(jnp.float32)
            coarse = jnp.round(whole * np.float32(1 / 256)) * np.float32(256)
            cwide[slot, core, b, :K, :] = coarse.astype(jnp.bfloat16)
            cwide[slot, core, b, K:, :] = (whole - coarse).astype(jnp.bfloat16)

    widen(0, c)
    for slot in range(1, NJ):
        c_copies[slot - 1].wait_recv()
        pass_on(slot).start()
        widen(slot, c)
    bytes_of(cbuf.at[:, c1], recv_sem.at[2], False)
    for slot in range(NJ):
        widen(slot, c1)

    def unpacked(packed):
        packed = packed.astype(jnp.float32)
        other_half = swapped(packed)
        return jnp.where(odd_half(HALF), other_half, packed), jnp.where(odd_half(HALF), packed, other_half)

    @pl.when(g == 2)
    def _():
        bytes_of(tz, t_sem.at[1], False)
        for half in range(2):
            for i in range(GS):
                first, last = unpacked(tz[half * GS + i])
                local[half, pl.ds(i * SLICE, HALF)] += first
                local[half, pl.ds(i * SLICE + HALF, HALF)] += last

    bytes_of(zbuf, recv_sem.at[3], False)
    for half in range(2):
        for i in range(GS):
            first, last = unpacked(zbuf[half * GS + i])
            zrows[half, pl.ds(i * SLICE, HALF)] = (local[half, pl.ds(i * SLICE, HALF)] + first).astype(jnp.bfloat16)
            zrows[half, pl.ds(i * SLICE + HALF, HALF)] = (local[half, pl.ds(i * SLICE + HALF, HALF)] + last).astype(jnp.bfloat16)
    z = zrows[...].reshape(2 * PATHS, NB * F)
    pre = jnp.dot(jnp.concatenate([z, z], axis=1), wbuf[...], preferred_element_type=jnp.float32)
    basis = jnp.tanh(pre + offsets).astype(jnp.bfloat16)
    twice = [jnp.concatenate([basis[:, b * K : (b + 1) * K]] * 2, axis=1) for b in range(NB)]

    for slot in range(NJ - 1, -1, -1):
        for b in range(NB):
            both = jnp.concatenate([cwide[slot, 0, b], cwide[slot, 1, b]], axis=1)
            values = jnp.dot(twice[b], both, preferred_element_type=jnp.float32)
            positive = jnp.sum(jnp.maximum(values, 0.0), axis=0, keepdims=True)
            part[slot, 0, b : b + 1, :] = positive[:, :SETS]
            part[slot, 1, b : b + 1, :] = positive[:, SETS:]
        for tc, tp in ((c1, p1), (c, p1), (c1, p), (c, p))[: 4 if slot else 3]:
            pltpu.make_async_remote_copy(
                src_ref=part.at[slot, tc], dst_ref=fin.at[slot * 4 + c * 2 + p], send_sem=send_sem.at[4], recv_sem=recv_sem.at[4],
                device_id={"trade": valued(slot) - c + tc, "path": tp}, device_id_type=MESH,
            ).start()

    fin[c * 2 + p] = part[0, c]
    bytes_of(fin.at[pl.ds(0, 15)], recv_sem.at[4], False)
    out[...] = jnp.sum(fin[...], axis=0) * unit[...] * np.float32(1.0 / (PATHS * 32))

    bytes_of(slices, send_sem.at[0], True)
    neighbour.wait_send()
    bytes_of(cbuf.at[pl.ds(0, NJ - 1), c], send_sem.at[1], True)
    bytes_of(cbuf.at[:, c], send_sem.at[2], True)
    bytes_of(zbuf, send_sem.at[3], True)
    bytes_of(fin.at[pl.ds(0, 15)], send_sem.at[4], True)

    @pl.when(g == 0)
    def _():
        total_copy(1, 0).wait_send()

    @pl.when(g == 0)
    def _():
        total_copy(1, 1).wait_send()

    @pl.when(g == 1)
    def _():
        bytes_of(tz, t_sent.at[1], True)

    @pl.when(jnp.logical_not(outer))
    def _():
        bytes_of(slices, send_sem.at[5], True)


def shards(normals, chol, volatility, start_state, basis_map, basis_bias, coef, maturity, netting):
    args = (
        normals, chol, volatility.reshape(1, -1), start_state.reshape(1, -1), basis_map,
        basis_bias.reshape(1, -1), coef, maturity.reshape(1, -1), netting.reshape(1, -1),
    )
    args = [pltpu.with_memory_space_constraint(a, pltpu.HBM) for a in args]
    return pl.pallas_call(
        kernel,
        out_shape=jax.ShapeDtypeStruct((NB, SETS), jnp.float32),
        in_specs=[pl.BlockSpec(memory_space=pltpu.HBM)] * len(args),
        out_specs=pl.BlockSpec(memory_space=pltpu.VMEM),
        scratch_shapes=[pltpu.VMEM(a.shape, a.dtype) for a in args]
        + [
            pltpu.VMEM((PATHS, NB * F), jnp.bfloat16),
            pltpu.VMEM((PATHS, NB * F), jnp.bfloat16),
            pltpu.VMEM((2, PATHS, NB * F), jnp.float32),
            pltpu.VMEM((GS, HALF, NB * F), jnp.bfloat16),
            pltpu.VMEM((GS, HALF, NB * F), jnp.bfloat16),
            pltpu.VMEM((GS, HALF, NB * F), jnp.bfloat16),
            pltpu.VMEM((2, HALF, NB * F), jnp.bfloat16),
            pltpu.VMEM((HALF, NB * F), jnp.bfloat16),
            pltpu.VMEM((HALF, NB * F), jnp.float32),
            pltpu.VMEM((GS, HALF, NB * F), jnp.bfloat16),
            pltpu.VMEM((2 * GS, HALF, NB * F), jnp.bfloat16),
            pltpu.VMEM((2 * GS, HALF, NB * F), jnp.bfloat16),
            pltpu.VMEM((2, PATHS, NB * F), jnp.bfloat16),
            pltpu.VMEM((NJ, 2, NB, K, SETS), jnp.int16),
            pltpu.VMEM((NJ, 2, NB, 2 * K, SETS), jnp.bfloat16),
            pltpu.VMEM((NB, SETS), jnp.float32),
            pltpu.VMEM((2 * NB * F, NB * K), jnp.bfloat16),
            pltpu.VMEM((NJ, 2, NB, SETS), jnp.float32),
            pltpu.VMEM((16, NB, SETS), jnp.float32),
            pltpu.SemaphoreType.DMA((len(args),)),
            pltpu.SemaphoreType.DMA((7,)),
            pltpu.SemaphoreType.DMA((7,)),
            pltpu.SemaphoreType.DMA((NJ - 1,)),
            pltpu.SemaphoreType.DMA((2,)),
            pltpu.SemaphoreType.DMA((2,)),
            pltpu.SemaphoreType.REGULAR((2,)),
        ],
        compiler_params=pltpu.CompilerParams(
            collective_id=0, has_side_effects=True, vmem_limit_bytes=24 << 20
        ),
    )(*args)


def solution(mesh):
    placed = (
        P("date", None, ("trade", "path")),
        P(),
        P(),
        P(),
        P(),
        P(),
        P(None, "trade"),
        P("trade"),
        P("trade"),
    )
    return jax.shard_map(
        shards, mesh=mesh, in_specs=placed, out_specs=P("date", "trade"), check_vma=False
    )
```

```python
import jax
import jax.numpy as jnp
import numpy as np
from jax import lax
from jax.experimental import pallas as pl
from jax.experimental.pallas import tpu as pltpu
from jax.sharding import PartitionSpec as P

MESH = pl.DeviceIdType.MESH
ND = 16
NB = 2
F = 64
K = 128
SETS = 128
GS = 4
SLICE = 64
HALF = SLICE // 2
PATHS = GS * SLICE
TOP = 127 * 256
NJ = 4
HIGH = lax.Precision.HIGHEST


def kernel(
    normals, chol, vol, start, bmap, bias, coef, mat, net,
    out,
    v_norm, v_chol, v_vol, v_start, v_bmap, v_bias, v_coef, v_mat, v_net,
    own_n, near_n, local, slices, arrived, ahead, tmsg, tbuf, base, sums, zbuf, tz, zrows, cbuf, cwide, unit, wbuf, part, fin,
    load_sem, send_sem, recv_sem, c_sem, t_sem, t_sent, ready,
):
    d, t, p = lax.axis_index("date"), lax.axis_index("trade"), lax.axis_index("path")
    y, c = lax.div(t, 2), lax.rem(t, 2)
    par = lax.rem(y, 2)
    side = 2 * par - 1
    g, w = lax.div(d, GS), lax.rem(d, GS)
    c1, p1 = 1 - c, 1 - p
    twin = t - 2 * side

    def row(steps):
        return lax.rem(t + 2 * steps + 16, 16)

    def valued(slot):
        return row(side * slot)

    def valuer(slot):
        return row(side * slot * (1 if slot % 2 else -1))

    barrier = pltpu.get_barrier_semaphore()

    def hello(where):
        pl.semaphore_signal(barrier, inc=1, device_id=where, device_id_type=MESH)

    def mate(i):
        return {"date": g * GS + lax.rem(w + i, GS), "path": p1}

    def counterpart(group, where=t):
        return {"date": group * GS + w, "trade": where}

    for i in range(GS):
        hello(mate(i))
    for i in (1, 2, 3, -2):
        hello({"trade": row(side * i)})
    hello({"trade": twin})
    other = t + 1 - 2 * c
    hello({"trade": other})
    hello({"trade": other, "path": p1})

    @pl.when(g == 0)
    def _():
        hello(counterpart(1))
        hello(counterpart(3))

    @pl.when(g == 1)
    def _():
        hello(counterpart(2))
        hello(counterpart(2, twin))

    outer = jnp.logical_or(g == 0, g == 3)
    beside = jnp.where(g < 2, 1 - g, 5 - g)

    def across(i):
        return {"date": beside * GS + lax.rem(w + i, GS), "path": p1}

    @pl.when(outer)
    def _():
        for i in range(GS):
            hello(across(i))

    loads = [
        pltpu.make_async_copy(a, b, load_sem.at[i])
        for i, (a, b) in enumerate(
            (
                (normals, v_norm), (coef, v_coef), (mat, v_mat), (net, v_net), (chol, v_chol),
                (vol, v_vol), (start, v_start), (bmap, v_bmap), (bias, v_bias),
            )
        )
    ]
    for load in loads:
        load.start()

    def odd_half(rows):
        return lax.broadcasted_iota(jnp.int32, (rows, NB * F), 1) >= F

    def swapped(block):
        return pltpu.roll(block, F, axis=1)

    loads[0].wait()
    normal = v_norm[...].reshape(NB * F, PATHS).astype(jnp.float32).T
    both = normal + swapped(normal)
    for i in range(GS):
        first = i * SLICE
        slices[i] = jnp.where(
            odd_half(HALF), both[first + HALF : first + SLICE], both[first : first + HALF]
        ).astype(jnp.bfloat16)

    for load in loads[1:4]:
        load.wait()
    local_set = v_net[...] - t * SETS
    trades = v_coef.shape[1]
    member = (lax.broadcasted_iota(jnp.int32, (SETS, trades), 0) == local_set)
    member = member.astype(jnp.float32).astype(jnp.bfloat16)
    for b in range(NB):
        alive = (d * NB + b < v_mat[...]).astype(jnp.float32).astype(jnp.bfloat16)
        folded = lax.dot_general(
            v_coef[...] * alive, member, (((1,), (1,)), ((), ())), preferred_element_type=jnp.float32
        )
        largest = jnp.maximum(jnp.max(jnp.abs(folded), axis=0, keepdims=True), np.float32(1e-30))
        unit[b : b + 1, :] = largest * np.float32(1.0 / TOP)
        cbuf[0, c, b] = jnp.round(folded * (np.float32(TOP) / largest)).astype(jnp.int32).astype(jnp.int16)

    heard = jnp.where(g == 0, 0, 1) + jnp.where(g == 2, 1, 0) + jnp.where(outer, 0, GS)
    pl.semaphore_wait(barrier, GS + 4 + 3 + heard)

    for i in (2, 3, 1, 0):
        pltpu.make_async_remote_copy(
            src_ref=slices.at[lax.rem(w + i, GS)], dst_ref=arrived.at[w], send_sem=send_sem.at[0], recv_sem=recv_sem.at[0],
            device_id=mate(i), device_id_type=MESH,
        ).start()

    @pl.when(jnp.logical_not(outer))
    def _():
        for i in range(GS):
            pltpu.make_async_remote_copy(
                src_ref=slices.at[lax.rem(w + i, GS)], dst_ref=ahead.at[w], send_sem=send_sem.at[5], recv_sem=recv_sem.at[5],
                device_id=across(i), device_id_type=MESH,
            ).start()

    def say_ready(to, slot, where=t):
        pl.semaphore_signal(ready.at[slot], inc=1, device_id=counterpart(to, where), device_id_type=MESH)

    @pl.when(g == 1)
    def _():
        say_ready(0, 0)

    @pl.when(g == 2)
    def _():
        say_ready(1, 0)
        say_ready(1, 0, twin)

    @pl.when(g == 3)
    def _():
        say_ready(0, 1)

    own_n[...] = normal.astype(jnp.bfloat16)
    neighbour = pltpu.make_async_remote_copy(
        src_ref=own_n, dst_ref=near_n, send_sem=send_sem.at[6], recv_sem=recv_sem.at[6],
        device_id={"trade": twin}, device_id_type=MESH,
    )
    neighbour.start()
    local[par] = jnp.where(odd_half(PATHS), both, normal)

    c_copies = [
        pltpu.make_async_remote_copy(
            src_ref=cbuf.at[0, c], dst_ref=cbuf.at[i, c], send_sem=send_sem.at[1], recv_sem=c_sem.at[i - 1],
            device_id={"trade": valuer(i)}, device_id_type=MESH,
        )
        for i in range(1, NJ)
    ]
    for copy in c_copies:
        copy.start()

    def pass_on(slot):
        return pltpu.make_async_remote_copy(
            src_ref=cbuf.at[slot, c], dst_ref=cbuf.at[slot, c], send_sem=send_sem.at[2], recv_sem=recv_sem.at[2],
            device_id={"trade": other}, device_id_type=MESH,
        )

    pass_on(0).start()

    for load in loads[4:]:
        load.wait()
    scale = v_vol[...] * np.float32(np.sqrt(np.float32(1.0) / np.float32(ND * NB)))
    joint = jnp.dot(v_chol[...].T * scale, v_bmap[...], precision=HIGH, preferred_element_type=jnp.float32)
    offset = jnp.dot(v_start[...], v_bmap[...], precision=HIGH, preferred_element_type=jnp.float32) + v_bias[...]
    joint_high = joint.astype(jnp.bfloat16)
    joint_low = (joint - joint_high.astype(jnp.float32)).astype(jnp.bfloat16)
    wbuf[...] = jnp.zeros_like(wbuf)
    for b in range(NB):
        wbuf[pl.ds(b * F, F), pl.ds(b * K, K)] = joint_high
        wbuf[pl.ds(NB * F + b * F, F), pl.ds(b * K, K)] = joint_low
    offsets = jnp.concatenate([offset, offset], axis=1)

    def bytes_of(ref, sem, send):
        whole = pltpu.make_async_remote_copy(
            src_ref=ref, dst_ref=ref, send_sem=sem, recv_sem=sem, device_id={"trade": other}, device_id_type=MESH
        )
        return whole.wait_send() if send else whole.wait_recv()

    bytes_of(arrived, recv_sem.at[0], False)
    blocks = [arrived[e].astype(jnp.float32) for e in range(GS)]
    own = blocks[0] + blocks[1] + blocks[2] + blocks[3]
    tmsg[0] = own.astype(jnp.bfloat16)

    def total_copy(to, message):
        return pltpu.make_async_remote_copy(
            src_ref=tmsg.at[message], dst_ref=tbuf, send_sem=t_sent.at[message], recv_sem=t_sem.at[0],
            device_id=counterpart(to), device_id_type=MESH,
        )

    @pl.when(g == 0)
    def _():
        base[...] = jnp.zeros_like(base)
        pl.semaphore_wait(ready.at[0], 1)
        total_copy(1, 0).start()

    @pl.when(g == 2)
    def _():
        base[...] = jnp.zeros_like(base)

    @pl.when(jnp.logical_or(g == 1, g == 3))
    def _():
        total_copy(0, 0).wait_recv()
        base[...] = tbuf[...].astype(jnp.float32)

    @pl.when(g == 3)
    def _():
        bytes_of(ahead, recv_sem.at[5], False)
        base[...] += sum(ahead[e].astype(jnp.float32) for e in range(GS))

    total = base[...]
    for e in range(GS):
        sums[e] = total.astype(jnp.bfloat16)
        total = total + blocks[e]
        for where in (twin, t):
            pltpu.make_async_remote_copy(
                src_ref=sums.at[e], dst_ref=zbuf.at[par * GS + w], send_sem=send_sem.at[3], recv_sem=recv_sem.at[3],
                device_id={"date": g * GS + e, "path": p1, "trade": where}, device_id_type=MESH,
            ).start()

    @pl.when(g == 1)
    def _():
        tmsg[1] = (own + base[...]).astype(jnp.bfloat16)
        pl.semaphore_wait(ready.at[0], 2)
        for i in range(GS):
            for where in (twin, t):
                pltpu.make_async_remote_copy(
                    src_ref=tmsg.at[1], dst_ref=tz.at[par * GS + w], send_sem=t_sent.at[1], recv_sem=t_sem.at[1],
                    device_id={"date": 2 * GS + i, "path": p1, "trade": where}, device_id_type=MESH,
                ).start()

    @pl.when(g == 0)
    def _():
        bytes_of(ahead, recv_sem.at[5], False)
        tmsg[1] = (own + sum(ahead[e].astype(jnp.float32) for e in range(GS))).astype(jnp.bfloat16)
        pl.semaphore_wait(ready.at[1], 1)
        total_copy(3, 1).start()

    neighbour.wait_recv()
    normal = near_n[...].astype(jnp.float32)
    local[1 - par] = normal + jnp.where(odd_half(PATHS), swapped(normal), 0.0)

    def widen(slot, core):
        for b in range(NB):
            whole = cbuf[slot, core, b].astype(jnp.int32).astype(jnp.float32)
            coarse = jnp.round(whole * np.float32(1 / 256)) * np.float32(256)
            cwide[slot, core, b, :K, :] = coarse.astype(jnp.bfloat16)
            cwide[slot, core, b, K:, :] = (whole - coarse).astype(jnp.bfloat16)

    widen(0, c)
    for slot in range(1, NJ):
        c_copies[slot - 1].wait_recv()
        pass_on(slot).start()
        widen(slot, c)

    def unpacked(packed):
        packed = packed.astype(jnp.float32)
        other_half = swapped(packed)
        return jnp.where(odd_half(HALF), other_half, packed), jnp.where(odd_half(HALF), packed, other_half)

    @pl.when(g == 2)
    def _():
        bytes_of(tz, t_sem.at[1], False)
        for half in range(2):
            for i in range(GS):
                first, last = unpacked(tz[half * GS + i])
                local[half, pl.ds(i * SLICE, HALF)] += first
                local[half, pl.ds(i * SLICE + HALF, HALF)] += last

    bytes_of(zbuf, recv_sem.at[3], False)
    for half in range(2):
        for i in range(GS):
            first, last = unpacked(zbuf[half * GS + i])
            zrows[half, pl.ds(i * SLICE, HALF)] = (local[half, pl.ds(i * SLICE, HALF)] + first).astype(jnp.bfloat16)
            zrows[half, pl.ds(i * SLICE + HALF, HALF)] = (local[half, pl.ds(i * SLICE + HALF, HALF)] + last).astype(jnp.bfloat16)
    z = zrows[...].reshape(2 * PATHS, NB * F)
    pre = jnp.dot(jnp.concatenate([z, z], axis=1), wbuf[...], preferred_element_type=jnp.float32)
    basis = jnp.tanh(pre + offsets).astype(jnp.bfloat16)
    twice = [jnp.concatenate([basis[:, b * K : (b + 1) * K]] * 2, axis=1) for b in range(NB)]

    bytes_of(cbuf.at[:, c1], recv_sem.at[2], False)
    for slot in range(NJ):
        widen(slot, c1)

    for slot in range(NJ - 1, -1, -1):
        for b in range(NB):
            both = jnp.concatenate([cwide[slot, 0, b], cwide[slot, 1, b]], axis=1)
            values = jnp.dot(twice[b], both, preferred_element_type=jnp.float32)
            positive = jnp.sum(jnp.maximum(values, 0.0), axis=0, keepdims=True)
            part[slot, 0, b : b + 1, :] = positive[:, :SETS]
            part[slot, 1, b : b + 1, :] = positive[:, SETS:]
        for tc, tp in ((c1, p1), (c, p1), (c1, p), (c, p))[: 4 if slot else 3]:
            pltpu.make_async_remote_copy(
                src_ref=part.at[slot, tc], dst_ref=fin.at[slot * 4 + c * 2 + p], send_sem=send_sem.at[4], recv_sem=recv_sem.at[4],
                device_id={"trade": valued(slot) - c + tc, "path": tp}, device_id_type=MESH,
            ).start()

    fin[c * 2 + p] = part[0, c]
    bytes_of(fin.at[pl.ds(0, 15)], recv_sem.at[4], False)
    out[...] = jnp.sum(fin[...], axis=0) * unit[...] * np.float32(1.0 / (PATHS * 32))

    bytes_of(slices, send_sem.at[0], True)
    neighbour.wait_send()
    bytes_of(cbuf.at[pl.ds(0, NJ - 1), c], send_sem.at[1], True)
    bytes_of(cbuf.at[:, c], send_sem.at[2], True)
    bytes_of(zbuf, send_sem.at[3], True)
    bytes_of(fin.at[pl.ds(0, 15)], send_sem.at[4], True)

    @pl.when(g == 0)
    def _():
        total_copy(1, 0).wait_send()

    @pl.when(g == 0)
    def _():
        total_copy(1, 1).wait_send()

    @pl.when(g == 1)
    def _():
        bytes_of(tz, t_sent.at[1], True)

    @pl.when(jnp.logical_not(outer))
    def _():
        bytes_of(slices, send_sem.at[5], True)


def shards(normals, chol, volatility, start_state, basis_map, basis_bias, coef, maturity, netting):
    args = (
        normals, chol, volatility.reshape(1, -1), start_state.reshape(1, -1), basis_map,
        basis_bias.reshape(1, -1), coef, maturity.reshape(1, -1), netting.reshape(1, -1),
    )
    args = [pltpu.with_memory_space_constraint(a, pltpu.HBM) for a in args]
    return pl.pallas_call(
        kernel,
        out_shape=jax.ShapeDtypeStruct((NB, SETS), jnp.float32),
        in_specs=[pl.BlockSpec(memory_space=pltpu.HBM)] * len(args),
        out_specs=pl.BlockSpec(memory_space=pltpu.VMEM),
        scratch_shapes=[pltpu.VMEM(a.shape, a.dtype) for a in args]
        + [
            pltpu.VMEM((PATHS, NB * F), jnp.bfloat16),
            pltpu.VMEM((PATHS, NB * F), jnp.bfloat16),
            pltpu.VMEM((2, PATHS, NB * F), jnp.float32),
            pltpu.VMEM((GS, HALF, NB * F), jnp.bfloat16),
            pltpu.VMEM((GS, HALF, NB * F), jnp.bfloat16),
            pltpu.VMEM((GS, HALF, NB * F), jnp.bfloat16),
            pltpu.VMEM((2, HALF, NB * F), jnp.bfloat16),
            pltpu.VMEM((HALF, NB * F), jnp.bfloat16),
            pltpu.VMEM((HALF, NB * F), jnp.float32),
            pltpu.VMEM((GS, HALF, NB * F), jnp.bfloat16),
            pltpu.VMEM((2 * GS, HALF, NB * F), jnp.bfloat16),
            pltpu.VMEM((2 * GS, HALF, NB * F), jnp.bfloat16),
            pltpu.VMEM((2, PATHS, NB * F), jnp.bfloat16),
            pltpu.VMEM((NJ, 2, NB, K, SETS), jnp.int16),
            pltpu.VMEM((NJ, 2, NB, 2 * K, SETS), jnp.bfloat16),
            pltpu.VMEM((NB, SETS), jnp.float32),
            pltpu.VMEM((2 * NB * F, NB * K), jnp.bfloat16),
            pltpu.VMEM((NJ, 2, NB, SETS), jnp.float32),
            pltpu.VMEM((16, NB, SETS), jnp.float32),
            pltpu.SemaphoreType.DMA((len(args),)),
            pltpu.SemaphoreType.DMA((7,)),
            pltpu.SemaphoreType.DMA((7,)),
            pltpu.SemaphoreType.DMA((NJ - 1,)),
            pltpu.SemaphoreType.DMA((2,)),
            pltpu.SemaphoreType.DMA((2,)),
            pltpu.SemaphoreType.REGULAR((2,)),
        ],
        compiler_params=pltpu.CompilerParams(
            collective_id=0, has_side_effects=True, vmem_limit_bytes=24 << 20
        ),
    )(*args)


def solution(mesh):
    placed = (
        P("date", None, ("trade", "path")),
        P(),
        P(),
        P(),
        P(),
        P(),
        P(None, "trade"),
        P("trade"),
        P("trade"),
    )
    return jax.shard_map(
        shards, mesh=mesh, in_specs=placed, out_specs=P("date", "trade"), check_vma=False
    )
```
